512 devices in a mesh: pair: 128 (over x, z, y_lo), col: 4 (over y_hi, core).
Axes of the slice: x: 4, y: 4 (y_hi: 2, y_lo: 2; y = y_hi * 2 + y_lo), z: 16, core: 2. Of those that a mesh axis runs over, the one named last changes fastest.
Arguments:
- amplitudes: bfloat16 [640, 512, 512], P('pair', None, 'col'), may hold values from -6 to 6
- fock_left: bfloat16 [512, 512], replicated, may hold values from -0.25 to 0.25
- dress_left: bfloat16 [512, 512], replicated, may hold values from -0.25 to 0.25
- fock_right: bfloat16 [512, 512], P(None, 'col'), may hold values from -0.25 to 0.25
- dress_right: bfloat16 [512, 512], P(None, 'col'), may hold values from -0.25 to 0.25
- hole_ladder: bfloat16 [576, 576], replicated, may hold values from -0.25 to 0.25
- slot_pair: int32 [640], replicated, may hold values from 0 to 639, as said below
- partner: int32 [640], replicated, may hold values from 0 to 639, as said below
- occ_energy: float32 [24], replicated, may hold values from -2 to -0.5
- virt_energy: float32 [512], replicated, may hold values from 0.3 to 3
- virt_order: int32 [512], replicated, may hold values from 0 to 511, each once
Outputs:
- update: float32 [640, 512, 512], P('pair', None, 'col')
The draws below stay inside these ranges and needn't reach their ends.
Inputs may be any that keep to these rules, and one draw needn't show every extreme that they name: slot_pair is a permutation of 0 to 639; values of 576 or more mark empty slots. partner[s] is the slot whose pair is (j, i) when slot s holds pair (i, j) = i * 24 + j; an empty slot is its own partner.
All inputs are finite; a program needn't handle non-finite values.
Results may differ from the reference program's by a relative error of at most 0.0033.
Values may be sent and summed in bfloat16 or wider, within the bound.
No kernel may reach another device: no remote copies, remote signals or barrier semaphores. Data moves between devices by JAX's collectives and lax.ppermute only.
A program may use at most 64 MiB of HBM per device.

```python
import jax
import jax.numpy as jnp
from jax import lax

O = 24
V = 512
PAIRS = 576
SLOT_DEV = 5
SLOTS = 640
N_PAIR = 128


def slot_perm(key):
    return jax.random.permutation(jax.random.fold_in(key, 11), SLOTS).astype(jnp.int32)


def draw_slot_pair(key, part):
    return slot_perm(key)


def draw_partner(key, part):
    perm = slot_perm(key)
    first = perm // O
    second = perm % O
    mirrored = jnp.where(perm < PAIRS, second * O + first, perm).astype(jnp.int32)
    inverse = jnp.argsort(perm).astype(jnp.int32)
    return inverse[mirrored].astype(jnp.int32)


def shard_levels(stream_key, extent, pieces, least, top_value):
    factor_of, own = 1.0, jax.random.fold_in(stream_key, 6)
    for position, shards_of in pieces:
        heights = jnp.exp(jax.random.uniform(jax.random.fold_in(own, position), (shards_of,), jnp.float32, least / len(pieces), top_value / len(pieces)))
        factor_of = factor_of * jnp.repeat(heights, extent[position] // shards_of).reshape([-1 if axis == position else 1 for axis in range(len(extent))])
    return factor_of


def scatter_about(rng, shape, spread, limit, shards=(), held_as=jnp.bfloat16):
    values = spread * jax.random.normal(rng, shape, jnp.float32)
    if shards:
        values = values * shard_levels(rng, shape, shards, -0.22, 0.18)
    return jnp.clip(values, -limit, limit).astype(held_as)


def setup_inputs(seed: int = 0) -> dict:
    keys = jax.random.split(jax.random.key(seed), 12)
    return {
        "amplitudes": scatter_about(keys[0], (SLOTS, V, V), 1.0, 6.0, ((0, 128), (2, 4))),
        "fock_left": scatter_about(keys[1], (V, V), V ** -0.5, 0.25),
        "dress_left": scatter_about(keys[2], (V, V), V ** -0.5, 0.25),
        "fock_right": scatter_about(keys[3], (V, V), V ** -0.5, 0.25, ((1, 4),)),
        "dress_right": scatter_about(keys[4], (V, V), V ** -0.5, 0.25, ((1, 4),)),
        "hole_ladder": scatter_about(keys[5], (PAIRS, PAIRS), PAIRS ** -0.5, 0.25),
        "slot_pair": draw_slot_pair(jax.random.fold_in(keys[11], 71), 0),
        "partner": draw_partner(jax.random.fold_in(keys[11], 71), 0),
        "occ_energy": jnp.clip(jax.random.uniform(keys[8], (O,), jnp.float32, -2.0, -0.5), -2.0, -0.5),
        "virt_energy": jnp.clip(jax.random.uniform(keys[9], (V,), jnp.float32, 0.3, 3.0), 0.3, 3.0),
        "virt_order": jax.random.permutation(keys[10], V).astype(jnp.int32),
    }


def wide_dot(left, right):
    return jnp.dot(left.astype(jnp.float32), right.astype(jnp.float32), precision=lax.Precision.HIGHEST, preferred_element_type=jnp.float32)


def reference(amplitudes, fock_left, dress_left, fock_right, dress_right, hole_ladder, slot_pair, partner, occ_energy, virt_energy, virt_order):
    def particle_block(amp):
        count = amp.shape[0]
        rows = amp.reshape(count * V, V)
        dressed = wide_dot(rows, dress_right).astype(jnp.bfloat16)
        right_part = wide_dot(rows, fock_right).reshape(count, V, V)
        amp_cols = jnp.transpose(amp, (1, 0, 2)).reshape(V, count * V)
        dressed_cols = jnp.transpose(dressed.reshape(count, V, V), (1, 0, 2)).reshape(V, count * V)
        left_part = wide_dot(fock_left, amp_cols)
        left_part = left_part + wide_dot(dress_left, dressed_cols)
        left_part = jnp.transpose(left_part.reshape(V, count, V), (1, 0, 2))
        return (left_part + right_part).astype(jnp.bfloat16)

    blocks = amplitudes.reshape(N_PAIR, SLOT_DEV, V, V)
    particle = lax.map(particle_block, blocks).reshape(SLOTS, V, V)
    padded = jnp.pad(hole_ladder, ((0, SLOTS - PAIRS), (0, SLOTS - PAIRS)))
    ladder_w = padded[slot_pair][:, slot_pair]
    flat = amplitudes.reshape(SLOTS, V * V)
    ladder = wide_dot(ladder_w, flat).astype(jnp.bfloat16).reshape(SLOTS, V, V)
    total = particle.astype(jnp.float32) + ladder.astype(jnp.float32)
    total = total + jnp.transpose(particle[partner], (0, 2, 1)).astype(jnp.float32)
    total = total + jnp.transpose(ladder[partner], (0, 2, 1)).astype(jnp.float32)
    live = slot_pair < PAIRS
    occ_first = jnp.minimum(slot_pair // O, O - 1).astype(jnp.int32)
    occ_second = (slot_pair % O).astype(jnp.int32)
    occ_sum = jnp.where(live, occ_energy[occ_first] + occ_energy[occ_second], jnp.zeros_like(occ_energy[occ_second]))
    energies = virt_energy[virt_order]
    denom = energies[None, :, None] + energies[None, None, :] - occ_sum[:, None, None]
    return total / denom
```

```python
import functools

import jax
import jax.numpy as jnp
from jax import lax
from jax.experimental import pallas as pl
from jax.experimental.pallas import tpu as pltpu
from jax.sharding import PartitionSpec as P

F32 = jnp.float32
BF16 = jnp.bfloat16


def dot(left, right):
    return jnp.dot(left, right, preferred_element_type=F32)


def chunks_of(total):
    return [(start, min(8, total - start)) for start in range(0, total, 8)]


def swap_rows(values, bits, first_bit, lanes):
    for step in range(bits):
        take = ((lax.broadcasted_iota(jnp.int32, values[0].shape, 1) >> (first_bit + step)) & 1) == 1
        bit = 1 << step
        values = [jnp.where(take, values[i ^ bit], values[i]) for i in range(len(values))]
    return values


def split_bits(nb):
    total = nb.bit_length() - 1
    low = (total + 1) // 2
    return low, total - low


def skew(source, middle, target, nb, count):
    low, high = split_bits(nb)
    for start, size in chunks_of(count):
        for base in range(1 << high):
            rows = [(base << low) + i for i in range(1 << low)]
            values = [source[pl.ds(start * nb + r, size, stride=nb), :] for r in rows]
            for r, value in zip(rows, swap_rows(values, low, 0, nb)):
                middle[r, start : start + size, :] = value
        for base in range(1 << low):
            rows = [base + (i << low) for i in range(1 << high)]
            values = [middle[r, start : start + size, :] for r in rows]
            for r, value in zip(rows, swap_rows(values, high, low, nb)):
                target[r * count + start : r * count + start + size, :] = value


def unskew(source, middle, target, nb, count):
    low, high = split_bits(nb)
    for start, size in chunks_of(count):
        for base in range(1 << low):
            rows = [base + (i << low) for i in range(1 << high)]
            values = [source[r * count + start : r * count + start + size, :] for r in rows]
            for r, value in zip(rows, swap_rows(values, high, low, nb)):
                middle[r, start : start + size, :] = value
        for base in range(1 << high):
            rows = [(base << low) + i for i in range(1 << low)]
            values = [middle[r, start : start + size, :] for r in rows]
            for r, value in zip(rows, swap_rows(values, low, 0, nb)):
                target[pl.ds(start * nb + r, size, stride=nb), :] = value


def skew_kernel(a_ref, out_ref, flat, middle, target):
    count = a_ref.shape[0] * (a_ref.shape[1] // a_ref.shape[2])
    nb = a_ref.shape[2]
    flat[...] = a_ref[...].reshape(count * nb, nb).astype(F32)
    skew(flat, middle, target, nb, count)
    out_ref[...] = target[...].astype(BF16)


def skew_scratch(count, nb):
    return [
        pltpu.VMEM((count * nb, nb), F32),
        pltpu.VMEM((nb, -(-count // 8) * 8, nb), F32),
        pltpu.VMEM((count * nb, nb), F32),
    ]


def weights_kernel(pair_col, pair_row, partner_col, h_ref, w_ref, w2_ref):
    slots = w_ref.shape[0]
    npairs = h_ref.shape[0]
    pick = (pair_col[...] == lax.broadcasted_iota(jnp.int32, (slots, npairs), 1)).astype(BF16)
    pick_t = (pair_row[...] == lax.broadcasted_iota(jnp.int32, (npairs, slots), 0)).astype(BF16)
    half = dot(pick, h_ref[...]).astype(BF16)
    w = dot(half, pick_t).astype(BF16)
    w_ref[...] = w
    mirror = (partner_col[...] == lax.broadcasted_iota(jnp.int32, (slots, slots), 1)).astype(BF16)
    w2_ref[...] = dot(mirror, w).astype(BF16)


def particle_kernel(
    c_ref, g0, g1, g2, g3, fl_ref, dl_ref, p_ref, out_ref, acat, dmat, fmat, flat, middle, target
):
    parts = (g0, g1, g2, g3)
    ncol = len(parts)
    nslot, nvirt, nb = p_ref.shape
    col = c_ref[0]
    for i in range(ncol):
        rows = pl.ds(pl.multiple_of((col ^ i) * nb, nb), nb)
        for k in range(ncol):
            fmat[i * nb : (i + 1) * nb, k * nb : (k + 1) * nb] = parts[k][nslot, rows, :]
            dmat[i * nb : (i + 1) * nb, k * nb : (k + 1) * nb] = parts[k][nslot + 1, rows, :]
    own = pl.ds(pl.multiple_of(col * nb, nb), nb)
    fl_own = fl_ref[own, :]
    dl_own = dl_ref[own, :]
    for s in range(nslot):
        for k in range(ncol):
            acat[:, k * nb : (k + 1) * nb] = parts[k][s]
        amp = acat[...]
        dressed = dot(amp, dmat[...]).astype(BF16)
        own_cols = dot(amp, fmat[:, :nb])
        own_cols = own_cols + dot(fl_ref[...], amp[:, :nb]) + dot(dl_ref[...], dressed[:, :nb])
        p_ref[s] = own_cols.astype(BF16)
        own_rows = dot(acat[own, :], fmat[...]) + dot(fl_own, amp) + dot(dl_own, dressed)
        own_rows = own_rows.astype(BF16).astype(F32)
        for k in range(ncol):
            at = pl.multiple_of((s * ncol + (col ^ k)) * nb, nb)
            flat[pl.ds(at, nb), :] = own_rows[:, k * nb : (k + 1) * nb].T
    skew(flat, middle, target, nb, nslot * ncol)
    out_ref[...] = target[...].astype(BF16)


def ladder_kernel(c_ref, j_ref, x_ref, w_ref, w2_ref, l_ref, m0, m1, m2, m3, wide, xcat, mirror):
    slots = w_ref.shape[0]
    nb = x_ref.shape[1]
    ncol = x_ref.shape[0] // slots
    wide[...] = x_ref[...].astype(F32)
    for d in range(ncol):
        xcat[:, d * nb : (d + 1) * nb] = wide[pl.ds(d, slots, stride=ncol), :].astype(BF16)
    l_ref[...] = dot(w_ref[...], xcat[...]).astype(BF16)
    other = dot(w2_ref[...], xcat[...]).astype(BF16)
    rows = lax.broadcasted_iota(jnp.int32, (nb, nb), 0)
    cols = lax.broadcasted_iota(jnp.int32, (nb, nb), 1)
    flip = (rows == (cols ^ j_ref[0])).astype(BF16)
    for d in range(ncol):
        mirror[d] = dot(other[:, d * nb : (d + 1) * nb], flip).astype(BF16)
    col = c_ref[0]
    for k, out in enumerate((m0, m1, m2, m3)):
        out[...] = mirror[col ^ k]


def combine_kernel(c_ref, y_ref, l_ref, m0, m1, m2, m3, partner_col, out_ref, wide, ycat, mirror):
    slots = l_ref.shape[0]
    nb = y_ref.shape[1]
    ncol = y_ref.shape[0] // slots
    wide[...] = y_ref[...].astype(F32)
    for d in range(ncol):
        ycat[:, d * nb : (d + 1) * nb] = wide[pl.ds(d, slots, stride=ncol), :].astype(BF16)
    pick = (partner_col[...] == lax.broadcasted_iota(jnp.int32, (slots, slots), 1)).astype(BF16)
    total = dot(pick, ycat[...]) + l_ref[...].astype(F32)
    col = c_ref[0]
    for k, part in enumerate((m0, m1, m2, m3)):
        mirror[col ^ k] = part[...]
    for d in range(ncol):
        wide[pl.ds(d, slots, stride=ncol), :] = total[:, d * nb : (d + 1) * nb] + mirror[d].astype(F32)
    out_ref[...] = wide[...].astype(BF16)


def finish_kernel(occ_ref, z_ref, p_ref, base_ref, out_ref, flat, middle, target):
    nslot, nvirt, nb = p_ref.shape
    flat[...] = z_ref[...].astype(F32)
    unskew(flat, middle, target, nb, nslot * (nvirt // nb))
    for s in range(nslot):
        total = p_ref[s].astype(F32) + target[s * nvirt : (s + 1) * nvirt, :]
        out_ref[s] = total / (base_ref[...] - occ_ref[s])


SMEM = pl.BlockSpec(memory_space=pltpu.SMEM)
VMEM = pl.BlockSpec(memory_space=pltpu.VMEM)


def call(kernel, outs, scratch, specs, name):
    return pl.pallas_call(
        kernel,
        out_shape=outs,
        in_specs=specs,
        out_specs=jax.tree.map(lambda _: VMEM, outs),
        scratch_shapes=scratch,
        name=name,
        compiler_params=pltpu.CompilerParams(vmem_limit_bytes=48 << 20),
    )


def body(
    amplitudes,
    fock_left,
    dress_left,
    fock_right,
    dress_right,
    hole_ladder,
    slot_pair,
    partner,
    occ_energy,
    virt_energy,
    virt_order,
):
    slot_dev, nvirt, nb = amplitudes.shape
    slots = slot_pair.shape[0]
    npairs = hole_ladder.shape[0]
    nocc = occ_energy.shape[0]
    ncol = nvirt // nb
    count = slot_dev * ncol
    col = lax.axis_index("col")
    pair = lax.axis_index("pair")
    col_s = jnp.reshape(col, (1,)).astype(jnp.int32)
    pair_s = jnp.reshape(pair, (1,)).astype(jnp.int32)
    shape = jax.ShapeDtypeStruct

    def exchange(rows):
        sent = rows.reshape(nb * slot_dev, ncol, nb)
        got = lax.all_to_all(sent, "pair", split_axis=0, concat_axis=0, tiled=True)
        return got.reshape(nb * count, nb)

    def swap(value, k):
        return lax.ppermute(value, "col", [(i, i ^ k) for i in range(ncol)])

    own = jnp.concatenate([amplitudes, fock_right[None], dress_right[None]])
    far = swap(own, 2)
    near = swap(own, 1)
    both = swap(far, 1)
    skewed = call(
        skew_kernel, shape((nb * count, nb), BF16), skew_scratch(count, nb), [VMEM], "skew"
    )(amplitudes)
    x = exchange(skewed)
    pair_col = slot_pair.reshape(slots, 1)
    pair_row = slot_pair.reshape(1, slots)
    partner_col = partner.reshape(slots, 1)
    w, w2 = call(
        weights_kernel, [shape((slots, slots), BF16)] * 2, [], [VMEM] * 4, "weights"
    )(pair_col, pair_row, partner_col, hole_ladder)
    particle, particle_rows = call(
        particle_kernel,
        [shape(amplitudes.shape, BF16), shape((nb * count, nb), BF16)],
        [pltpu.VMEM((nvirt, nvirt), BF16)] * 3 + skew_scratch(count, nb),
        [SMEM] + [VMEM] * 6,
        "particle",
    )(col_s, own, near, far, both, fock_left, dress_left)
    y = exchange(particle_rows)
    ladder, m0, m1, m2, m3 = call(
        ladder_kernel,
        [shape((slots, nvirt), BF16)] + [shape((slots, nb), BF16)] * 4,
        [
            pltpu.VMEM((slots * ncol, nb), F32),
            pltpu.VMEM((slots, nvirt), BF16),
            pltpu.VMEM((ncol, slots, nb), BF16),
        ],
        [SMEM] * 2 + [VMEM] * 3,
        "ladder",
    )(col_s, pair_s, x, w, w2)
    m1, m2, m3 = swap(m1, 1), swap(m2, 2), swap(m3, 3)
    back = call(
        combine_kernel,
        shape((nb * count, nb), BF16),
        [
            pltpu.VMEM((slots * ncol, nb), F32),
            pltpu.VMEM((slots, nvirt), BF16),
            pltpu.VMEM((ncol, slots, nb), BF16),
        ],
        [SMEM] + [VMEM] * 7,
        "combine",
    )(col_s, y, ladder, m0, m1, m2, m3, partner_col)
    z = exchange(back)
    own_pairs = lax.dynamic_slice_in_dim(slot_pair, pair * slot_dev, slot_dev)
    occ_iota = jnp.arange(nocc, dtype=jnp.int32)
    first_hot = (own_pairs[:, None] // nocc == occ_iota[None, :]).astype(F32)
    second_hot = (own_pairs[:, None] % nocc == occ_iota[None, :]).astype(F32)
    live = (own_pairs < npairs).astype(F32)
    occ_sum = live * (
        jnp.sum(first_hot * occ_energy[None, :], axis=1)
        + jnp.sum(second_hot * occ_energy[None, :], axis=1)
    )
    virt_iota = jnp.arange(nvirt, dtype=jnp.int32)
    row_hot = (virt_order[:, None] == virt_iota[None, :]).astype(F32)
    row_energy = jnp.sum(row_hot * virt_energy[None, :], axis=1)
    col_energy = lax.dynamic_slice_in_dim(row_energy, col * nb, nb)
    base = row_energy[:, None] + col_energy[None, :]
    return call(
        finish_kernel,
        shape(amplitudes.shape, F32),
        skew_scratch(count, nb),
        [SMEM] + [VMEM] * 3,
        "finish",
    )(occ_sum, z, particle, base)


def solution(mesh):
    placed = (
        P("pair", None, "col"),
        P(),
        P(),
        P(None, "col"),
        P(None, "col"),
        P(),
        P(),
        P(),
        P(),
        P(),
        P(),
    )
    return jax.shard_map(
        body, mesh=mesh, in_specs=placed, out_specs=P("pair", None, "col"), check_vma=False
    )
```

```python
import jax
import jax.numpy as jnp
from jax import lax
from jax.experimental import pallas as pl
from jax.experimental.pallas import tpu as pltpu
from jax.sharding import PartitionSpec as P

F32 = jnp.float32
BF16 = jnp.bfloat16


def dot(left, right):
    return jnp.dot(left, right, preferred_element_type=F32)


def chunks_of(total):
    return [(start, min(8, total - start)) for start in range(0, total, 8)]


def swap_rows(values, bits, first_bit):
    for step in range(bits):
        take = ((lax.broadcasted_iota(jnp.int32, values[0].shape, 1) >> (first_bit + step)) & 1) == 1
        bit = 1 << step
        values = [jnp.where(take, values[i ^ bit], values[i]) for i in range(len(values))]
    return values


def split_bits(nb):
    total = nb.bit_length() - 1
    low = (total + 1) // 2
    return low, total - low


def skew(source, middle, target, nb, count):
    low, high = split_bits(nb)
    for start, size in chunks_of(count):
        for base in range(1 << high):
            rows = [(base << low) + i for i in range(1 << low)]
            values = [source[pl.ds(start * nb + r, size, stride=nb), :] for r in rows]
            for r, value in zip(rows, swap_rows(values, low, 0)):
                middle[r, start : start + size, :] = value
        for base in range(1 << low):
            rows = [base + (i << low) for i in range(1 << high)]
            values = [middle[r, start : start + size, :] for r in rows]
            for r, value in zip(rows, swap_rows(values, high, low)):
                target[r * count + start : r * count + start + size, :] = value


def unskew(source, middle, target, nb, count):
    low, high = split_bits(nb)
    for start, size in chunks_of(count):
        for base in range(1 << low):
            rows = [base + (i << low) for i in range(1 << high)]
            values = [source[r * count + start : r * count + start + size, :] for r in rows]
            for r, value in zip(rows, swap_rows(values, high, low)):
                middle[r, start : start + size, :] = value
        for base in range(1 << high):
            rows = [(base << low) + i for i in range(1 << low)]
            values = [middle[r, start : start + size, :] for r in rows]
            for r, value in zip(rows, swap_rows(values, low, 0)):
                target[pl.ds(start * nb + r, size, stride=nb), :] = value


def skew_kernel(a_ref, out_ref, flat, middle, target):
    count = a_ref.shape[0] * (a_ref.shape[1] // a_ref.shape[2])
    nb = a_ref.shape[2]
    flat[...] = a_ref[...].reshape(count * nb, nb).astype(F32)
    skew(flat, middle, target, nb, count)
    out_ref[...] = target[...].astype(BF16)


def skew_scratch(count, nb):
    return [
        pltpu.VMEM((count * nb, nb), F32),
        pltpu.VMEM((nb, -(-count // 8) * 8, nb), F32),
        pltpu.VMEM((count * nb, nb), F32),
    ]


def weights_kernel(pair_col, pair_row, partner_col, h_ref, w_ref, w2_ref):
    slots = w_ref.shape[0]
    npairs = h_ref.shape[0]
    pick = (pair_col[...] == lax.broadcasted_iota(jnp.int32, (slots, npairs), 1)).astype(BF16)
    pick_t = (pair_row[...] == lax.broadcasted_iota(jnp.int32, (npairs, slots), 0)).astype(BF16)
    half = dot(pick, h_ref[...]).astype(BF16)
    w = dot(half, pick_t).astype(BF16)
    w_ref[...] = w
    mirror = (partner_col[...] == lax.broadcasted_iota(jnp.int32, (slots, slots), 1)).astype(BF16)
    w2_ref[...] = dot(mirror, w).astype(BF16)


def particle_kernel(
    c_ref, g0, g1, g2, g3, fl_ref, dl_ref, p_ref, out_ref, acat, dmat, fmat, flat, middle, target
):
    parts = (g0, g1, g2, g3)
    ncol = len(parts)
    nslot, _, nb = p_ref.shape
    col = c_ref[0]
    for i in range(ncol):
        rows = pl.ds(pl.multiple_of((col ^ i) * nb, nb), nb)
        for k in range(ncol):
            fmat[i * nb : (i + 1) * nb, k * nb : (k + 1) * nb] = parts[k][nslot, rows, :]
            dmat[i * nb : (i + 1) * nb, k * nb : (k + 1) * nb] = parts[k][nslot + 1, rows, :]
    own = pl.ds(pl.multiple_of(col * nb, nb), nb)
    fl_own = fl_ref[own, :]
    dl_own = dl_ref[own, :]
    for s in range(nslot):
        for k in range(ncol):
            acat[:, k * nb : (k + 1) * nb] = parts[k][s]
        amp = acat[...]
        dressed = dot(amp, dmat[...]).astype(BF16)
        own_cols = dot(amp, fmat[:, :nb])
        own_cols = own_cols + dot(fl_ref[...], amp[:, :nb]) + dot(dl_ref[...], dressed[:, :nb])
        p_ref[s] = own_cols.astype(BF16)
        own_rows = dot(acat[own, :], fmat[...]) + dot(fl_own, amp) + dot(dl_own, dressed)
        own_rows = own_rows.astype(BF16).astype(F32)
        for k in range(ncol):
            at = pl.multiple_of((s * ncol + (col ^ k)) * nb, nb)
            flat[pl.ds(at, nb), :] = own_rows[:, k * nb : (k + 1) * nb].T
    skew(flat, middle, target, nb, nslot * ncol)
    out_ref[...] = target[...].astype(BF16)


def ladder_kernel(c_ref, j_ref, x_ref, w_ref, w2_ref, l_ref, m0, m1, m2, m3, wide, xcat, mirror):
    slots = w_ref.shape[0]
    nb = x_ref.shape[1]
    ncol = x_ref.shape[0] // slots
    wide[...] = x_ref[...].astype(F32)
    for d in range(ncol):
        xcat[:, d * nb : (d + 1) * nb] = wide[pl.ds(d, slots, stride=ncol), :].astype(BF16)
    l_ref[...] = dot(w_ref[...], xcat[...]).astype(BF16)
    other = dot(w2_ref[...], xcat[...]).astype(BF16)
    rows = lax.broadcasted_iota(jnp.int32, (nb, nb), 0)
    cols = lax.broadcasted_iota(jnp.int32, (nb, nb), 1)
    flip = (rows == (cols ^ j_ref[0])).astype(BF16)
    for d in range(ncol):
        mirror[d] = dot(other[:, d * nb : (d + 1) * nb], flip).astype(BF16)
    col = c_ref[0]
    for k, out in enumerate((m0, m1, m2, m3)):
        out[...] = mirror[col ^ k]


def combine_kernel(c_ref, y_ref, l_ref, m0, m1, m2, m3, partner_col, out_ref, wide, ycat, mirror):
    slots = l_ref.shape[0]
    nb = y_ref.shape[1]
    ncol = y_ref.shape[0] // slots
    wide[...] = y_ref[...].astype(F32)
    for d in range(ncol):
        ycat[:, d * nb : (d + 1) * nb] = wide[pl.ds(d, slots, stride=ncol), :].astype(BF16)
    pick = (partner_col[...] == lax.broadcasted_iota(jnp.int32, (slots, slots), 1)).astype(BF16)
    total = dot(pick, ycat[...]) + l_ref[...].astype(F32)
    col = c_ref[0]
    for k, part in enumerate((m0, m1, m2, m3)):
        mirror[col ^ k] = part[...]
    for d in range(ncol):
        wide[pl.ds(d, slots, stride=ncol), :] = total[:, d * nb : (d + 1) * nb] + mirror[d].astype(F32)
    out_ref[...] = wide[...].astype(BF16)


def finish_kernel(occ_ref, z_ref, p_ref, base_ref, out_ref, flat, middle, target):
    nslot, nvirt, nb = p_ref.shape
    flat[...] = z_ref[...].astype(F32)
    unskew(flat, middle, target, nb, nslot * (nvirt // nb))
    for s in range(nslot):
        total = p_ref[s].astype(F32) + target[s * nvirt : (s + 1) * nvirt, :]
        out_ref[s] = total / (base_ref[...] - occ_ref[s])


SMEM = pl.BlockSpec(memory_space=pltpu.SMEM)
VMEM = pl.BlockSpec(memory_space=pltpu.VMEM)


def call(kernel, outs, scratch, specs):
    return pl.pallas_call(
        kernel,
        out_shape=outs,
        in_specs=specs,
        out_specs=jax.tree.map(lambda _: VMEM, outs),
        scratch_shapes=scratch,
        compiler_params=pltpu.CompilerParams(vmem_limit_bytes=20 << 20),
    )


def update_of(
    amplitudes,
    fock_left,
    dress_left,
    fock_right,
    dress_right,
    hole_ladder,
    slot_pair,
    partner,
    occ_energy,
    virt_energy,
    virt_order,
):
    slot_dev, nvirt, nb = amplitudes.shape
    slots = slot_pair.shape[0]
    npairs = hole_ladder.shape[0]
    nocc = occ_energy.shape[0]
    ncol = nvirt // nb
    count = slot_dev * ncol
    col = lax.axis_index("col")
    pair = lax.axis_index("pair")
    col_s = jnp.reshape(col, (1,)).astype(jnp.int32)
    pair_s = jnp.reshape(pair, (1,)).astype(jnp.int32)
    shape = jax.ShapeDtypeStruct

    def exchange(rows):
        sent = rows.reshape(nb * slot_dev, ncol, nb)
        got = lax.all_to_all(sent, "pair", split_axis=0, concat_axis=0, tiled=True)
        return got.reshape(nb * count, nb)

    def swap(value, k):
        return lax.ppermute(value, "col", [(i, i ^ k) for i in range(ncol)])

    own = jnp.concatenate([amplitudes, fock_right[None], dress_right[None]])
    far = swap(own, 2)
    near = swap(own, 1)
    both = swap(far, 1)
    skewed = call(
        skew_kernel, shape((nb * count, nb), BF16), skew_scratch(count, nb), [VMEM]
    )(amplitudes)
    x = exchange(skewed)
    pair_col = slot_pair.reshape(slots, 1)
    pair_row = slot_pair.reshape(1, slots)
    partner_col = partner.reshape(slots, 1)
    w, w2 = call(
        weights_kernel, [shape((slots, slots), BF16)] * 2, [], [VMEM] * 4
    )(pair_col, pair_row, partner_col, hole_ladder)
    particle, particle_rows = call(
        particle_kernel,
        [shape(amplitudes.shape, BF16), shape((nb * count, nb), BF16)],
        [pltpu.VMEM((nvirt, nvirt), BF16)] * 3 + skew_scratch(count, nb),
        [SMEM] + [VMEM] * 6,
    )(col_s, own, near, far, both, fock_left, dress_left)
    y = exchange(particle_rows)
    ladder, m0, m1, m2, m3 = call(
        ladder_kernel,
        [shape((slots, nvirt), BF16)] + [shape((slots, nb), BF16)] * 4,
        [
            pltpu.VMEM((slots * ncol, nb), F32),
            pltpu.VMEM((slots, nvirt), BF16),
            pltpu.VMEM((ncol, slots, nb), BF16),
        ],
        [SMEM] * 2 + [VMEM] * 3,
    )(col_s, pair_s, x, w, w2)
    m1, m2, m3 = swap(m1, 1), swap(m2, 2), swap(m3, 3)
    back = call(
        combine_kernel,
        shape((nb * count, nb), BF16),
        [
            pltpu.VMEM((slots * ncol, nb), F32),
            pltpu.VMEM((slots, nvirt), BF16),
            pltpu.VMEM((ncol, slots, nb), BF16),
        ],
        [SMEM] + [VMEM] * 7,
    )(col_s, y, ladder, m0, m1, m2, m3, partner_col)
    z = exchange(back)
    own_pairs = lax.dynamic_slice_in_dim(slot_pair, pair * slot_dev, slot_dev)
    occ_iota = jnp.arange(nocc, dtype=jnp.int32)
    first_hot = (own_pairs[:, None] // nocc == occ_iota[None, :]).astype(F32)
    second_hot = (own_pairs[:, None] % nocc == occ_iota[None, :]).astype(F32)
    live = (own_pairs < npairs).astype(F32)
    occ_sum = live * (
        jnp.sum(first_hot * occ_energy[None, :], axis=1)
        + jnp.sum(second_hot * occ_energy[None, :], axis=1)
    )
    virt_iota = jnp.arange(nvirt, dtype=jnp.int32)
    row_hot = (virt_order[:, None] == virt_iota[None, :]).astype(F32)
    row_energy = jnp.sum(row_hot * virt_energy[None, :], axis=1)
    col_energy = lax.dynamic_slice_in_dim(row_energy, col * nb, nb)
    base = row_energy[:, None] + col_energy[None, :]
    return call(
        finish_kernel, shape(amplitudes.shape, F32), skew_scratch(count, nb), [SMEM] + [VMEM] * 3
    )(occ_sum, z, particle, base)


def solution(mesh):
    placed = (
        P("pair", None, "col"),
        P(),
        P(),
        P(None, "col"),
        P(None, "col"),
        P(),
        P(),
        P(),
        P(),
        P(),
        P(),
    )
    return jax.shard_map(
        update_of, mesh=mesh, in_specs=placed, out_specs=P("pair", None, "col"), check_vma=False
    )
```

```python
import jax
import jax.numpy as jnp
from jax import lax
from jax.experimental import pallas as pl
from jax.experimental.pallas import tpu as pltpu
from jax.sharding import PartitionSpec as P

F32 = jnp.float32
BF16 = jnp.bfloat16


def dot(left, right):
    return jnp.dot(left, right, preferred_element_type=F32)


def chunks_of(total):
    return [(start, min(8, total - start)) for start in range(0, total, 8)]


def swap_rows(values, bits, first_bit):
    for step in range(bits):
        take = ((lax.broadcasted_iota(jnp.int32, values[0].shape, 1) >> (first_bit + step)) & 1) == 1
        bit = 1 << step
        values = [jnp.where(take, values[i ^ bit], values[i]) for i in range(len(values))]
    return values


def split_bits(nb):
    total = nb.bit_length() - 1
    low = (total + 1) // 2
    return low, total - low


def skew(source, middle, target, nb, count, ready):
    low, high = split_bits(nb)
    for start, size in chunks_of(count):
        ready(start, size)
        for base in range(1 << high):
            rows = [(base << low) + i for i in range(1 << low)]
            values = [source[pl.ds(start * nb + r, size, stride=nb), :] for r in rows]
            for r, value in zip(rows, swap_rows(values, low, 0)):
                middle[r, start : start + size, :] = value
        for base in range(1 << low):
            rows = [base + (i << low) for i in range(1 << high)]
            values = [middle[r, start : start + size, :] for r in rows]
            for r, value in zip(rows, swap_rows(values, high, low)):
                target[r * count + start : r * count + start + size, :] = value


def unskew(source, middle, target, nb, count, done):
    low, high = split_bits(nb)
    for start, size in chunks_of(count):
        for base in range(1 << low):
            rows = [base + (i << low) for i in range(1 << high)]
            values = [source[r * count + start : r * count + start + size, :] for r in rows]
            for r, value in zip(rows, swap_rows(values, high, low)):
                middle[r, start : start + size, :] = value
        for base in range(1 << high):
            rows = [(base << low) + i for i in range(1 << low)]
            values = [middle[r, start : start + size, :] for r in rows]
            for r, value in zip(rows, swap_rows(values, low, 0)):
                target[pl.ds(start * nb + r, size, stride=nb), :] = value
        done(start, size)


def skew_kernel(a_hbm, out_ref, raw, sems, flat, middle, target):
    nslot, nvirt, nb = raw.shape
    ncol = nvirt // nb
    copies = [pltpu.make_async_copy(a_hbm.at[s], raw.at[s], sems.at[s]) for s in range(nslot)]
    for copy in copies:
        copy.start()

    def ready(start, size):
        for s in range(start // ncol, (start + size) // ncol):
            copies[s].wait()
            flat[s * nvirt : (s + 1) * nvirt, :] = raw[s].astype(F32)

    skew(flat, middle, target, nb, nslot * ncol, ready)
    out_ref[...] = target[...].astype(BF16)


def skew_scratch(count, nb):
    return [
        pltpu.VMEM((count * nb, nb), F32),
        pltpu.VMEM((nb, -(-count // 8) * 8, nb), F32),
        pltpu.VMEM((count * nb, nb), F32),
    ]


def weights_kernel(pair_col, pair_row, partner_col, h_ref, w_ref, w2_ref):
    slots = w_ref.shape[0]
    npairs = h_ref.shape[0]
    pick = (pair_col[...] == lax.broadcasted_iota(jnp.int32, (slots, npairs), 1)).astype(BF16)
    pick_t = (pair_row[...] == lax.broadcasted_iota(jnp.int32, (npairs, slots), 0)).astype(BF16)
    half = dot(pick, h_ref[...]).astype(BF16)
    w = dot(half, pick_t).astype(BF16)
    w_ref[...] = w
    mirror = (partner_col[...] == lax.broadcasted_iota(jnp.int32, (slots, slots), 1)).astype(BF16)
    w2_ref[...] = dot(mirror, w).astype(BF16)


def gather_columns(parts, s, acat):
    nb = parts[0].shape[2]
    for k, part in enumerate(parts):
        acat[:, k * nb : (k + 1) * nb] = part[s]
    return acat[...]


def rows_kernel(
    c_ref, g0, g1, g2, g3, w0, w1, w2, w3, fl_ref, dl_ref, out_ref,
    left, right, acat, low, flat, middle, target,
):
    parts = (g0, g1, g2, g3)
    wide = (w0, w1, w2, w3)
    ncol = len(parts)
    nslot, nvirt, nb = g0.shape
    col = c_ref[0]
    own = pl.ds(pl.multiple_of(col * nb, nb), nb)
    left[:nb, :] = fl_ref[own, :]
    left[nb:, :] = dl_ref[own, :]
    for i in range(ncol):
        rows = pl.ds(pl.multiple_of((col ^ i) * nb, nb), nb)
        for k in range(ncol):
            right[i * nb : (i + 1) * nb, k * nb : (k + 1) * nb] = wide[k][1, rows, :]
            right[nvirt + i * nb : nvirt + (i + 1) * nb, k * nb : (k + 1) * nb] = wide[k][0, rows, :]

    def ready(start, size):
        for s in range(start // ncol, (start + size) // ncol):
            amp = gather_columns(parts, s, acat)
            first = dot(left[...], amp)
            low[:, :nvirt] = first[nb:].astype(BF16)
            for k, part in enumerate(parts):
                low[:, nvirt + k * nb : nvirt + (k + 1) * nb] = part[s, own, :]
            total = first[:nb] + dot(low[...], right[...])
            for k in range(ncol):
                at = pl.multiple_of((s * ncol + (col ^ k)) * nb, nb)
                flat[pl.ds(at, nb), :] = total[:, k * nb : (k + 1) * nb].T

    skew(flat, middle, target, nb, nslot * ncol, ready)
    out_ref[...] = target[...].astype(BF16)


def cols_kernel(c_ref, g0, g1, g2, g3, w0, fl_ref, dl_ref, p_ref, right, acat):
    parts = (g0, g1, g2, g3)
    ncol = len(parts)
    nslot, _, nb = g0.shape
    col = c_ref[0]
    for i in range(ncol):
        rows = pl.ds(pl.multiple_of((col ^ i) * nb, nb), nb)
        right[i * nb : (i + 1) * nb, :nb] = w0[1, rows, :]
        right[i * nb : (i + 1) * nb, nb:] = w0[0, rows, :]
    for s in range(nslot):
        amp = gather_columns(parts, s, acat)
        both = dot(amp, right[...])
        dressed = both[:, :nb].astype(BF16)
        total = both[:, nb:] + dot(fl_ref[...], g0[s]) + dot(dl_ref[...], dressed)
        p_ref[s] = total.astype(BF16)


def ladder_kernel(c_ref, j_ref, x_ref, w_ref, w2_ref, l_ref, m0, m1, m2, m3, wide, xcat, mirror):
    slots = w_ref.shape[0]
    nb = x_ref.shape[1]
    ncol = x_ref.shape[0] // slots
    wide[...] = x_ref[...].astype(F32)
    for d in range(ncol):
        xcat[:, d * nb : (d + 1) * nb] = wide[pl.ds(d, slots, stride=ncol), :].astype(BF16)
    l_ref[...] = dot(w_ref[...], xcat[...]).astype(BF16)
    other = dot(w2_ref[...], xcat[...]).astype(BF16)
    rows = lax.broadcasted_iota(jnp.int32, (nb, nb), 0)
    cols = lax.broadcasted_iota(jnp.int32, (nb, nb), 1)
    flip = (rows == (cols ^ j_ref[0])).astype(BF16)
    for d in range(ncol):
        mirror[d] = dot(other[:, d * nb : (d + 1) * nb], flip).astype(BF16)
    col = c_ref[0]
    for k, out in enumerate((m0, m1, m2, m3)):
        out[...] = mirror[col ^ k]


def combine_kernel(
    c_ref, y_ref, l_hbm, m0, m1, m2, m3, partner_col, out_ref, wide, ycat, mirror, l_ref, sems
):
    slots = l_ref.shape[0]
    nb = y_ref.shape[1]
    ncol = y_ref.shape[0] // slots
    col = c_ref[0]
    copies = [pltpu.make_async_copy(l_hbm, l_ref, sems.at[ncol])]
    for k, part in enumerate((m0, m1, m2, m3)):
        copies.append(pltpu.make_async_copy(part, mirror.at[col ^ k], sems.at[k]))
    for copy in copies:
        copy.start()
    wide[...] = y_ref[...].astype(F32)
    for d in range(ncol):
        ycat[:, d * nb : (d + 1) * nb] = wide[pl.ds(d, slots, stride=ncol), :].astype(BF16)
    pick = (partner_col[...] == lax.broadcasted_iota(jnp.int32, (slots, slots), 1)).astype(BF16)
    total = dot(pick, ycat[...])
    for copy in copies:
        copy.wait()
    for d in range(ncol):
        at = slice(d * nb, (d + 1) * nb)
        wide[pl.ds(d, slots, stride=ncol), :] = (
            total[:, at] + l_ref[:, at].astype(F32) + mirror[d].astype(F32)
        )
    out_ref[...] = wide[...].astype(BF16)


def finish_kernel(occ_ref, z_ref, p_ref, base_ref, out_hbm, stage, sems, flat, middle, target):
    nslot, nvirt, nb = p_ref.shape
    ncol = nvirt // nb
    flat[...] = z_ref[...].astype(F32)
    copies = [pltpu.make_async_copy(stage.at[s], out_hbm.at[s], sems.at[s]) for s in range(nslot)]

    def done(start, size):
        for s in range(start // ncol, (start + size) // ncol):
            total = p_ref[s].astype(F32) + target[s * nvirt : (s + 1) * nvirt, :]
            stage[s] = total / (base_ref[...] - occ_ref[s])
            copies[s].start()

    unskew(flat, middle, target, nb, nslot * ncol, done)
    for copy in copies:
        copy.wait()


SMEM = pl.BlockSpec(memory_space=pltpu.SMEM)
VMEM = pl.BlockSpec(memory_space=pltpu.VMEM)
HBM = pl.BlockSpec(memory_space=pltpu.HBM)


def stay(value):
    return pltpu.with_memory_space_constraint(value, pltpu.HBM)


def call(kernel, outs, scratch, specs, result=VMEM):
    return pl.pallas_call(
        kernel,
        out_shape=outs,
        in_specs=specs,
        out_specs=jax.tree.map(lambda _: result, outs),
        scratch_shapes=scratch,
        compiler_params=pltpu.CompilerParams(vmem_limit_bytes=20 << 20),
    )


def update_of(
    amplitudes,
    fock_left,
    dress_left,
    fock_right,
    dress_right,
    hole_ladder,
    slot_pair,
    partner,
    occ_energy,
    virt_energy,
    virt_order,
):
    slot_dev, nvirt, nb = amplitudes.shape
    slots = slot_pair.shape[0]
    npairs = hole_ladder.shape[0]
    nocc = occ_energy.shape[0]
    ncol = nvirt // nb
    count = slot_dev * ncol
    col = lax.axis_index("col")
    pair = lax.axis_index("pair")
    col_s = jnp.reshape(col, (1,)).astype(jnp.int32)
    pair_s = jnp.reshape(pair, (1,)).astype(jnp.int32)
    shape = jax.ShapeDtypeStruct

    def exchange(rows):
        sent = rows.reshape(nb * slot_dev, ncol, nb)
        got = lax.all_to_all(sent, "pair", split_axis=0, concat_axis=0, tiled=True)
        return got.reshape(nb * count, nb)

    def swap(value, k):
        return lax.ppermute(value, "col", [(i, i ^ k) for i in range(ncol)])

    far = swap(amplitudes, 2)
    dma = pltpu.SemaphoreType.DMA
    skewed = call(
        skew_kernel,
        shape((nb * count, nb), BF16),
        [pltpu.VMEM(amplitudes.shape, BF16), dma((slot_dev,))] + skew_scratch(count, nb),
        [HBM],
    )(stay(amplitudes))
    x = exchange(skewed)
    pair_col = slot_pair.reshape(slots, 1)
    pair_row = slot_pair.reshape(1, slots)
    partner_col = partner.reshape(slots, 1)
    w, w2 = call(
        weights_kernel, [shape((slots, slots), BF16)] * 2, [], [VMEM] * 4
    )(pair_col, pair_row, partner_col, hole_ladder)
    near = swap(amplitudes, 1)
    both = swap(far, 1)
    wide = jnp.stack([fock_right, dress_right])
    wide_far = swap(wide, 2)
    wide_near = swap(wide, 1)
    wide_both = swap(wide_far, 1)
    particle_rows = call(
        rows_kernel,
        shape((nb * count, nb), BF16),
        [
            pltpu.VMEM((2 * nb, nvirt), BF16),
            pltpu.VMEM((2 * nvirt, nvirt), BF16),
            pltpu.VMEM((nvirt, nvirt), BF16),
            pltpu.VMEM((nb, 2 * nvirt), BF16),
        ]
        + skew_scratch(count, nb),
        [SMEM] + [VMEM] * 10,
    )(
        col_s, amplitudes, near, far, both, wide, wide_near, wide_far, wide_both,
        fock_left, dress_left,
    )
    y = exchange(particle_rows)
    particle = call(
        cols_kernel,
        shape(amplitudes.shape, BF16),
        [pltpu.VMEM((nvirt, 2 * nb), BF16), pltpu.VMEM((nvirt, nvirt), BF16)],
        [SMEM] + [VMEM] * 7,
    )(col_s, amplitudes, near, far, both, wide, fock_left, dress_left)
    ladder, m0, m1, m2, m3 = call(
        ladder_kernel,
        [shape((slots, nvirt), BF16)] + [shape((slots, nb), BF16)] * 4,
        [
            pltpu.VMEM((slots * ncol, nb), F32),
            pltpu.VMEM((slots, nvirt), BF16),
            pltpu.VMEM((ncol, slots, nb), BF16),
        ],
        [SMEM] * 2 + [VMEM] * 3,
    )(col_s, pair_s, x, w, w2)
    m1, m2, m3 = swap(m1, 1), swap(m2, 2), swap(m3, 3)
    back = call(
        combine_kernel,
        shape((nb * count, nb), BF16),
        [
            pltpu.VMEM((slots * ncol, nb), F32),
            pltpu.VMEM((slots, nvirt), BF16),
            pltpu.VMEM((ncol, slots, nb), BF16),
            pltpu.VMEM((slots, nvirt), BF16),
            dma((ncol + 1,)),
        ],
        [SMEM, VMEM] + [HBM] * 5 + [VMEM],
    )(col_s, y, stay(ladder), stay(m0), stay(m1), stay(m2), stay(m3), partner_col)
    z = exchange(back)
    own_pairs = lax.dynamic_slice_in_dim(slot_pair, pair * slot_dev, slot_dev)
    occ_iota = jnp.arange(nocc, dtype=jnp.int32)
    first_hot = (own_pairs[:, None] // nocc == occ_iota[None, :]).astype(F32)
    second_hot = (own_pairs[:, None] % nocc == occ_iota[None, :]).astype(F32)
    live = (own_pairs < npairs).astype(F32)
    occ_sum = live * (
        jnp.sum(first_hot * occ_energy[None, :], axis=1)
        + jnp.sum(second_hot * occ_energy[None, :], axis=1)
    )
    virt_iota = jnp.arange(nvirt, dtype=jnp.int32)
    row_hot = (virt_order[:, None] == virt_iota[None, :]).astype(F32)
    row_energy = jnp.sum(row_hot * virt_energy[None, :], axis=1)
    col_energy = lax.dynamic_slice_in_dim(row_energy, col * nb, nb)
    base = row_energy[:, None] + col_energy[None, :]
    return call(
        finish_kernel,
        shape(amplitudes.shape, F32),
        [pltpu.VMEM(amplitudes.shape, F32), dma((slot_dev,))] + skew_scratch(count, nb),
        [SMEM] + [VMEM] * 3,
        HBM,
    )(occ_sum, z, particle, base)


def solution(mesh):
    placed = (
        P("pair", None, "col"),
        P(),
        P(),
        P(None, "col"),
        P(None, "col"),
        P(),
        P(),
        P(),
        P(),
        P(),
        P(),
    )
    return jax.shard_map(
        update_of, mesh=mesh, in_specs=placed, out_specs=P("pair", None, "col"), check_vma=False
    )
```

```python
import jax
import jax.numpy as jnp
from jax import lax
from jax.experimental import pallas as pl
from jax.experimental.pallas import tpu as pltpu
from jax.sharding import PartitionSpec as P

F32 = jnp.float32
BF16 = jnp.bfloat16


def dot(left, right):
    return jnp.dot(left, right, preferred_element_type=F32)


def chunks_of(total):
    return [(start, min(8, total - start)) for start in range(0, total, 8)]


def swap_rows(values, bits, first_bit):
    for step in range(bits):
        take = ((lax.broadcasted_iota(jnp.int32, values[0].shape, 1) >> (first_bit + step)) & 1) == 1
        bit = 1 << step
        values = [jnp.where(take, values[i ^ bit], values[i]) for i in range(len(values))]
    return values


def split_bits(nb):
    total = nb.bit_length() - 1
    low = (total + 1) // 2
    return low, total - low


def skew(source, middle, target, nb, count, ready):
    low, high = split_bits(nb)
    for start, size in chunks_of(count):
        ready(start, size)
        for base in range(1 << high):
            rows = [(base << low) + i for i in range(1 << low)]
            values = [source[pl.ds(start * nb + r, size, stride=nb), :] for r in rows]
            for r, value in zip(rows, swap_rows(values, low, 0)):
                middle[r, start : start + size, :] = value
        for base in range(1 << low):
            rows = [base + (i << low) for i in range(1 << high)]
            values = [middle[r, start : start + size, :] for r in rows]
            for r, value in zip(rows, swap_rows(values, high, low)):
                target[r * count + start : r * count + start + size, :] = value


def unskew(source, middle, target, nb, count, done):
    low, high = split_bits(nb)
    for start, size in chunks_of(count):
        for base in range(1 << low):
            rows = [base + (i << low) for i in range(1 << high)]
            values = [source[r * count + start : r * count + start + size, :] for r in rows]
            for r, value in zip(rows, swap_rows(values, high, low)):
                middle[r, start : start + size, :] = value
        for base in range(1 << high):
            rows = [(base << low) + i for i in range(1 << low)]
            values = [middle[r, start : start + size, :] for r in rows]
            for r, value in zip(rows, swap_rows(values, low, 0)):
                target[pl.ds(start * nb + r, size, stride=nb), :] = value
        done(start, size)


def skew_kernel(a_ref, out_ref, flat, middle, target):
    nslot, nvirt, nb = a_ref.shape
    ncol = nvirt // nb

    def ready(start, size):
        for s in range(start // ncol, (start + size) // ncol):
            flat[s * nvirt : (s + 1) * nvirt, :] = a_ref[s].astype(F32)

    skew(flat, middle, target, nb, nslot * ncol, ready)
    out_ref[...] = target[...].astype(BF16)


def skew_scratch(count, nb):
    return [
        pltpu.VMEM((count * nb, nb), F32),
        pltpu.VMEM((nb, -(-count // 8) * 8, nb), F32),
        pltpu.VMEM((count * nb, nb), F32),
    ]


def weights_kernel(pair_col, pair_row, partner_col, h_ref, w_ref, w2_ref):
    slots = w_ref.shape[0]
    npairs = h_ref.shape[0]
    pick = (pair_col[...] == lax.broadcasted_iota(jnp.int32, (slots, npairs), 1)).astype(BF16)
    pick_t = (pair_row[...] == lax.broadcasted_iota(jnp.int32, (npairs, slots), 0)).astype(BF16)
    half = dot(pick, h_ref[...]).astype(BF16)
    w = dot(half, pick_t).astype(BF16)
    w_ref[...] = w
    mirror = (partner_col[...] == lax.broadcasted_iota(jnp.int32, (slots, slots), 1)).astype(BF16)
    w2_ref[...] = dot(mirror, w).astype(BF16)


def gather_columns(parts, s, acat):
    nb = parts[0].shape[2]
    for k, part in enumerate(parts):
        acat[:, k * nb : (k + 1) * nb] = part[s]
    return acat[...]


def rows_kernel(
    c_ref, g0, g1, g2, g3, w0, w1, w2, w3, fl_ref, dl_ref, out_ref,
    left, dmat, fmat, stack, low, flat, middle, target,
):
    parts = (g0, g1, g2, g3)
    wide = (w0, w1, w2, w3)
    ncol = len(parts)
    nslot, nvirt, nb = g0.shape
    col = c_ref[0]
    own = pl.ds(pl.multiple_of(col * nb, nb), nb)
    left[:, :nvirt] = fl_ref[own, :]
    left[:, nvirt:] = dl_ref[own, :]
    for i in range(ncol):
        rows = pl.ds(pl.multiple_of((col ^ i) * nb, nb), nb)
        for k in range(ncol):
            at = (slice(i * nb, (i + 1) * nb), slice(k * nb, (k + 1) * nb))
            fmat[at] = wide[k][0, rows, :]
            dmat[at] = wide[k][1, rows, :]

    def ready(start, size):
        for s in range(start // ncol, (start + size) // ncol):
            for k, part in enumerate(parts):
                stack[:nvirt, k * nb : (k + 1) * nb] = part[s]
                low[:, k * nb : (k + 1) * nb] = part[s, own, :]
            stack[nvirt:, :] = dot(stack[:nvirt, :], dmat[...]).astype(BF16)
            total = dot(left[...], stack[...]) + dot(low[...], fmat[...])
            for k in range(ncol):
                at = pl.multiple_of((s * ncol + (col ^ k)) * nb, nb)
                flat[pl.ds(at, nb), :] = total[:, k * nb : (k + 1) * nb].T

    skew(flat, middle, target, nb, nslot * ncol, ready)
    out_ref[...] = target[...].astype(BF16)


def cols_kernel(c_ref, g0, g1, g2, g3, w0, fl_ref, dl_ref, p_ref, right, acat):
    parts = (g0, g1, g2, g3)
    ncol = len(parts)
    nslot, _, nb = g0.shape
    col = c_ref[0]
    for i in range(ncol):
        rows = pl.ds(pl.multiple_of((col ^ i) * nb, nb), nb)
        right[i * nb : (i + 1) * nb, :nb] = w0[1, rows, :]
        right[i * nb : (i + 1) * nb, nb:] = w0[0, rows, :]
    for s in range(nslot):
        amp = gather_columns(parts, s, acat)
        both = dot(amp, right[...])
        dressed = both[:, :nb].astype(BF16)
        total = both[:, nb:] + dot(fl_ref[...], g0[s]) + dot(dl_ref[...], dressed)
        p_ref[s] = total.astype(BF16)


def ladder_kernel(c_ref, j_ref, x_ref, w_ref, w2_ref, l_ref, m0, m1, m2, m3, wide, xcat, mirror):
    slots = w_ref.shape[0]
    nb = x_ref.shape[1]
    ncol = x_ref.shape[0] // slots
    wide[...] = x_ref[...].astype(F32)
    for d in range(ncol):
        xcat[:, d * nb : (d + 1) * nb] = wide[pl.ds(d, slots, stride=ncol), :].astype(BF16)
    plain = dot(w_ref[...], xcat[...])
    for d in range(ncol):
        l_ref[d] = plain[:, d * nb : (d + 1) * nb].astype(BF16)
    other = dot(w2_ref[...], xcat[...]).astype(BF16)
    rows = lax.broadcasted_iota(jnp.int32, (nb, nb), 0)
    cols = lax.broadcasted_iota(jnp.int32, (nb, nb), 1)
    flip = (rows == (cols ^ j_ref[0])).astype(BF16)
    for d in range(ncol):
        mirror[d] = dot(other[:, d * nb : (d + 1) * nb], flip).astype(BF16)
    col = c_ref[0]
    for k, out in enumerate((m0, m1, m2, m3)):
        out[...] = mirror[col ^ k]


def mirror_kernel(c_ref, l_ref, m0, m1, m2, m3, out_ref):
    col = c_ref[0]
    for k, part in enumerate((m0, m1, m2, m3)):
        out_ref[col ^ k] = (l_ref[col ^ k].astype(F32) + part[...].astype(F32)).astype(BF16)


def combine_kernel(y_ref, s_hbm, partner_col, out_ref, wide, ycat, both, sems):
    ncol, slots, nb = both.shape
    copies = [pltpu.make_async_copy(s_hbm.at[d], both.at[d], sems.at[d]) for d in range(ncol)]
    for copy in copies:
        copy.start()
    wide[...] = y_ref[...].astype(F32)
    for d in range(ncol):
        ycat[:, d * nb : (d + 1) * nb] = wide[pl.ds(d, slots, stride=ncol), :].astype(BF16)
    pick = (partner_col[...] == lax.broadcasted_iota(jnp.int32, (slots, slots), 1)).astype(BF16)
    total = dot(pick, ycat[...])
    for d in range(ncol):
        copies[d].wait()
        wide[pl.ds(d, slots, stride=ncol), :] = (
            total[:, d * nb : (d + 1) * nb] + both[d].astype(F32)
        )
    out_ref[...] = wide[...].astype(BF16)


def finish_kernel(occ_ref, z_ref, p_ref, base_ref, out_hbm, stage, sems, flat, middle, target):
    nslot, nvirt, nb = p_ref.shape
    ncol = nvirt // nb
    flat[...] = z_ref[...].astype(F32)
    copies = [pltpu.make_async_copy(stage.at[s], out_hbm.at[s], sems.at[s]) for s in range(nslot)]

    def done(start, size):
        for s in range(start // ncol, (start + size) // ncol):
            total = p_ref[s].astype(F32) + target[s * nvirt : (s + 1) * nvirt, :]
            stage[s] = total / (base_ref[...] - occ_ref[s])
            copies[s].start()

    unskew(flat, middle, target, nb, nslot * ncol, done)
    for copy in copies:
        copy.wait()


SMEM = pl.BlockSpec(memory_space=pltpu.SMEM)
VMEM = pl.BlockSpec(memory_space=pltpu.VMEM)
HBM = pl.BlockSpec(memory_space=pltpu.HBM)


def stay(value):
    return pltpu.with_memory_space_constraint(value, pltpu.HBM)


def call(kernel, outs, scratch, specs, result=VMEM):
    return pl.pallas_call(
        kernel,
        out_shape=outs,
        in_specs=specs,
        out_specs=jax.tree.map(lambda _: result, outs),
        scratch_shapes=scratch,
        compiler_params=pltpu.CompilerParams(vmem_limit_bytes=20 << 20),
    )


def update_of(
    amplitudes,
    fock_left,
    dress_left,
    fock_right,
    dress_right,
    hole_ladder,
    slot_pair,
    partner,
    occ_energy,
    virt_energy,
    virt_order,
):
    slot_dev, nvirt, nb = amplitudes.shape
    slots = slot_pair.shape[0]
    npairs = hole_ladder.shape[0]
    nocc = occ_energy.shape[0]
    ncol = nvirt // nb
    count = slot_dev * ncol
    col = lax.axis_index("col")
    pair = lax.axis_index("pair")
    col_s = jnp.reshape(col, (1,)).astype(jnp.int32)
    pair_s = jnp.reshape(pair, (1,)).astype(jnp.int32)
    shape = jax.ShapeDtypeStruct

    def exchange(rows):
        sent = rows.reshape(nb * slot_dev, ncol, nb)
        got = lax.all_to_all(sent, "pair", split_axis=0, concat_axis=0, tiled=True)
        return got.reshape(nb * count, nb)

    def swap(value, k):
        return lax.ppermute(value, "col", [(i, i ^ k) for i in range(ncol)])

    far = swap(amplitudes, 2)
    dma = pltpu.SemaphoreType.DMA
    skewed = call(
        skew_kernel, shape((nb * count, nb), BF16), skew_scratch(count, nb), [VMEM]
    )(amplitudes)
    x = exchange(skewed)
    pair_col = slot_pair.reshape(slots, 1)
    pair_row = slot_pair.reshape(1, slots)
    partner_col = partner.reshape(slots, 1)
    w, w2 = call(
        weights_kernel, [shape((slots, slots), BF16)] * 2, [], [VMEM] * 4
    )(pair_col, pair_row, partner_col, hole_ladder)
    near = swap(amplitudes, 1)
    both = swap(far, 1)
    wide = jnp.stack([fock_right, dress_right])
    wide_far = swap(wide, 2)
    wide_near = swap(wide, 1)
    wide_both = swap(wide_far, 1)
    particle_rows = call(
        rows_kernel,
        shape((nb * count, nb), BF16),
        [
            pltpu.VMEM((nb, 2 * nvirt), BF16),
            pltpu.VMEM((nvirt, nvirt), BF16),
            pltpu.VMEM((nvirt, nvirt), BF16),
            pltpu.VMEM((2 * nvirt, nvirt), BF16),
            pltpu.VMEM((nb, nvirt), BF16),
        ]
        + skew_scratch(count, nb),
        [SMEM] + [VMEM] * 10,
    )(
        col_s, amplitudes, near, far, both, wide, wide_near, wide_far, wide_both,
        fock_left, dress_left,
    )
    y = exchange(particle_rows)
    particle = call(
        cols_kernel,
        shape(amplitudes.shape, BF16),
        [pltpu.VMEM((nvirt, 2 * nb), BF16), pltpu.VMEM((nvirt, nvirt), BF16)],
        [SMEM] + [VMEM] * 7,
    )(col_s, amplitudes, near, far, both, wide, fock_left, dress_left)
    ladder, m0, m1, m2, m3 = call(
        ladder_kernel,
        [shape((ncol, slots, nb), BF16)] + [shape((slots, nb), BF16)] * 4,
        [
            pltpu.VMEM((slots * ncol, nb), F32),
            pltpu.VMEM((slots, nvirt), BF16),
            pltpu.VMEM((ncol, slots, nb), BF16),
        ],
        [SMEM] * 2 + [VMEM] * 3,
    )(col_s, pair_s, x, w, w2)
    m1, m2, m3 = swap(m1, 1), swap(m2, 2), swap(m3, 3)
    both_terms = call(
        mirror_kernel, shape((ncol, slots, nb), BF16), [], [SMEM] + [VMEM] * 5
    )(col_s, ladder, m0, m1, m2, m3)
    back = call(
        combine_kernel,
        shape((nb * count, nb), BF16),
        [
            pltpu.VMEM((slots * ncol, nb), F32),
            pltpu.VMEM((slots, nvirt), BF16),
            pltpu.VMEM((ncol, slots, nb), BF16),
            dma((ncol,)),
        ],
        [VMEM, HBM, VMEM],
    )(y, stay(both_terms), partner_col)
    z = exchange(back)
    own_pairs = lax.dynamic_slice_in_dim(slot_pair, pair * slot_dev, slot_dev)
    occ_iota = jnp.arange(nocc, dtype=jnp.int32)
    first_hot = (own_pairs[:, None] // nocc == occ_iota[None, :]).astype(F32)
    second_hot = (own_pairs[:, None] % nocc == occ_iota[None, :]).astype(F32)
    live = (own_pairs < npairs).astype(F32)
    occ_sum = live * (
        jnp.sum(first_hot * occ_energy[None, :], axis=1)
        + jnp.sum(second_hot * occ_energy[None, :], axis=1)
    )
    virt_iota = jnp.arange(nvirt, dtype=jnp.int32)
    row_hot = (virt_order[:, None] == virt_iota[None, :]).astype(F32)
    row_energy = jnp.sum(row_hot * virt_energy[None, :], axis=1)
    col_energy = lax.dynamic_slice_in_dim(row_energy, col * nb, nb)
    base = row_energy[:, None] + col_energy[None, :]
    return call(
        finish_kernel,
        shape(amplitudes.shape, F32),
        [pltpu.VMEM(amplitudes.shape, F32), dma((slot_dev,))] + skew_scratch(count, nb),
        [SMEM] + [VMEM] * 3,
        HBM,
    )(occ_sum, z, particle, base)


def solution(mesh):
    placed = (
        P("pair", None, "col"),
        P(),
        P(),
        P(None, "col"),
        P(None, "col"),
        P(),
        P(),
        P(),
        P(),
        P(),
        P(),
    )
    return jax.shard_map(
        update_of, mesh=mesh, in_specs=placed, out_specs=P("pair", None, "col"), check_vma=False
    )
```

```python
import jax
import jax.numpy as jnp
from jax import lax
from jax.experimental import pallas as pl
from jax.experimental.pallas import tpu as pltpu
from jax.sharding import PartitionSpec as P

F32 = jnp.float32
BF16 = jnp.bfloat16
PAD = 8


def dot(left, right):
    return jnp.dot(left, right, preferred_element_type=F32)


def chunks_of(total):
    return [(start, min(8, total - start)) for start in range(0, total, 8)]


def pitch_of(nb):
    return nb + PAD


def swap_rows(values, bits, first_bit):
    for step in range(bits):
        take = ((lax.broadcasted_iota(jnp.int32, values[0].shape, 1) >> (first_bit + step)) & 1) == 1
        bit = 1 << step
        values = [jnp.where(take, values[i ^ bit], values[i]) for i in range(len(values))]
    return values


def split_bits(nb):
    total = nb.bit_length() - 1
    low = (total + 1) // 2
    return low, total - low


def skew(source, middle, target, nb, count, ready, done):
    low, high = split_bits(nb)
    pitch = pitch_of(nb)
    for start, size in chunks_of(count):
        ready(start, size)
        for base in range(1 << low):
            rows = [base + (i << low) for i in range(1 << high)]
            values = [source[pl.ds(start * pitch + r, size, stride=pitch), :] for r in rows]
            for r, value in zip(rows, swap_rows(values, high, low)):
                middle[r, start : start + size, :] = value
    for base in range(1 << high):
        rows = [(base << low) + i for i in range(1 << low)]
        for start, size in chunks_of(count):
            values = [middle[r, start : start + size, :] for r in rows]
            for r, value in zip(rows, swap_rows(values, low, 0)):
                target[r * count + start : r * count + start + size, :] = value
        done(rows[0] * count, len(rows) * count)


def unskew(source, middle, target, nb, count, done):
    low, high = split_bits(nb)
    pitch = pitch_of(nb)
    for start, size in chunks_of(count):
        for base in range(1 << low):
            rows = [base + (i << low) for i in range(1 << high)]
            values = [source[r * count + start : r * count + start + size, :] for r in rows]
            for r, value in zip(rows, swap_rows(values, high, low)):
                middle[r, start : start + size, :] = value
        for base in range(1 << high):
            rows = [(base << low) + i for i in range(1 << low)]
            values = [middle[r, start : start + size, :] for r in rows]
            for r, value in zip(rows, swap_rows(values, low, 0)):
                target[pl.ds(start * pitch + r, size, stride=pitch), :] = value
        done(start, size)


def pieces(source, target, sems, count):
    size = source.shape[0] // count
    return [
        pltpu.make_async_copy(
            source.at[pl.ds(i * size, size)], target.at[pl.ds(i * size, size)], sems.at[i]
        )
        for i in range(count)
    ]


def skew_kernel(a_hbm, out_hbm, raw, packed, sems_in, sems_out, flat, middle, target):
    nslot, nvirt, nb = raw.shape
    ncol = nvirt // nb
    fetches = pieces(a_hbm, raw, sems_in, nslot)
    for copy in fetches:
        copy.start()
    stores = pieces(packed, out_hbm, sems_out, sems_out.shape[0])

    def ready(start, size):
        for s in range(start // ncol, (start + size) // ncol):
            fetches[s].wait()
            for d in range(ncol):
                at = (s * ncol + d) * pitch_of(nb)
                flat[at : at + nb, :] = raw[s, d * nb : (d + 1) * nb, :].astype(F32)

    def done(start, size):
        packed[start : start + size, :] = target[start : start + size, :].astype(BF16)
        stores[start // size].start()

    skew(flat, middle, target, nb, nslot * ncol, ready, done)
    for copy in stores:
        copy.wait()


def skew_scratch(count, nb):
    return [
        pltpu.VMEM((count * pitch_of(nb), nb), F32),
        pltpu.VMEM((nb, -(-count // 8) * 8, nb), F32),
        pltpu.VMEM((count * pitch_of(nb), nb), F32),
    ]


def weights_kernel(pair_col, pair_row, partner_col, h_ref, w_ref, w2_ref):
    slots = w_ref.shape[0]
    npairs = h_ref.shape[0]
    pick = (pair_col[...] == lax.broadcasted_iota(jnp.int32, (slots, npairs), 1)).astype(BF16)
    pick_t = (pair_row[...] == lax.broadcasted_iota(jnp.int32, (npairs, slots), 0)).astype(BF16)
    half = dot(pick, h_ref[...]).astype(BF16)
    w = dot(half, pick_t).astype(BF16)
    w_ref[...] = w
    mirror = (partner_col[...] == lax.broadcasted_iota(jnp.int32, (slots, slots), 1)).astype(BF16)
    w2_ref[...] = dot(mirror, w).astype(BF16)


def gather_columns(parts, s, acat):
    nb = parts[0].shape[2]
    for k, part in enumerate(parts):
        acat[:, k * nb : (k + 1) * nb] = part[s]
    return acat[...]


def rows_kernel(
    c_ref, g0, g1, g2, g3, w0, w1, w2, w3, fl_ref, dl_ref, out_ref,
    left, dmat, fmat, stack, low, flat, middle, target,
):
    parts = (g0, g1, g2, g3)
    wide = (w0, w1, w2, w3)
    ncol = len(parts)
    nslot, nvirt, nb = g0.shape
    col = c_ref[0]
    own = pl.ds(pl.multiple_of(col * nb, nb), nb)
    left[:, :nvirt] = fl_ref[own, :]
    left[:, nvirt:] = dl_ref[own, :]
    for i in range(ncol):
        rows = pl.ds(pl.multiple_of((col ^ i) * nb, nb), nb)
        for k in range(ncol):
            at = (slice(i * nb, (i + 1) * nb), slice(k * nb, (k + 1) * nb))
            fmat[at] = wide[k][0, rows, :]
            dmat[at] = wide[k][1, rows, :]

    def ready(start, size):
        for s in range(start // ncol, (start + size) // ncol):
            for k, part in enumerate(parts):
                stack[:nvirt, k * nb : (k + 1) * nb] = part[s]
                low[:, k * nb : (k + 1) * nb] = part[s, own, :]
            stack[nvirt:, :] = dot(stack[:nvirt, :], dmat[...]).astype(BF16)
            total = dot(left[...], stack[...]) + dot(low[...], fmat[...])
            for k in range(ncol):
                at = pl.multiple_of((s * ncol + (col ^ k)) * pitch_of(nb), 8)
                flat[pl.ds(at, nb), :] = total[:, k * nb : (k + 1) * nb].T

    def done(start, size):
        out_ref[start : start + size, :] = target[start : start + size, :].astype(BF16)

    skew(flat, middle, target, nb, nslot * ncol, ready, done)


def cols_kernel(c_ref, g0, g1, g2, g3, w0, fl_ref, dl_ref, p_ref, right, acat):
    parts = (g0, g1, g2, g3)
    ncol = len(parts)
    nslot, _, nb = g0.shape
    col = c_ref[0]
    for i in range(ncol):
        rows = pl.ds(pl.multiple_of((col ^ i) * nb, nb), nb)
        right[i * nb : (i + 1) * nb, :nb] = w0[1, rows, :]
        right[i * nb : (i + 1) * nb, nb:] = w0[0, rows, :]
    for s in range(nslot):
        amp = gather_columns(parts, s, acat)
        both = dot(amp, right[...])
        dressed = both[:, :nb].astype(BF16)
        total = both[:, nb:] + dot(fl_ref[...], g0[s]) + dot(dl_ref[...], dressed)
        p_ref[s] = total.astype(BF16)


def ladder_kernel(c_ref, j_ref, x_ref, w_ref, w2_ref, l_ref, m0, m1, m2, m3, wide, xcat, mirror):
    slots = w_ref.shape[0]
    nb = x_ref.shape[1]
    ncol = x_ref.shape[0] // slots
    wide[...] = x_ref[...].astype(F32)
    for d in range(ncol):
        xcat[:, d * nb : (d + 1) * nb] = wide[pl.ds(d, slots, stride=ncol), :].astype(BF16)
    plain = dot(w_ref[...], xcat[...])
    for d in range(ncol):
        l_ref[d] = plain[:, d * nb : (d + 1) * nb].astype(BF16)
    other = dot(w2_ref[...], xcat[...]).astype(BF16)
    rows = lax.broadcasted_iota(jnp.int32, (nb, nb), 0)
    cols = lax.broadcasted_iota(jnp.int32, (nb, nb), 1)
    flip = (rows == (cols ^ j_ref[0])).astype(BF16)
    for d in range(ncol):
        mirror[d] = dot(other[:, d * nb : (d + 1) * nb], flip).astype(BF16)
    col = c_ref[0]
    for k, out in enumerate((m0, m1, m2, m3)):
        out[...] = mirror[col ^ k]


def mirror_kernel(c_ref, l_ref, m0, m1, m2, m3, out_ref):
    col = c_ref[0]
    for k, part in enumerate((m0, m1, m2, m3)):
        out_ref[col ^ k] = (l_ref[col ^ k].astype(F32) + part[...].astype(F32)).astype(BF16)


def combine_kernel(
    y_ref, s_hbm, partner_col, out_hbm, wide, ycat, both, packed, sems_in, sems_out
):
    ncol, slots, nb = both.shape
    fetches = pieces(s_hbm, both, sems_in, ncol)
    for copy in fetches:
        copy.start()
    stores = pieces(packed, out_hbm, sems_out, sems_out.shape[0])
    wide[...] = y_ref[...].astype(F32)
    for d in range(ncol):
        ycat[:, d * nb : (d + 1) * nb] = wide[pl.ds(d, slots, stride=ncol), :].astype(BF16)
    pick = partner_col[...] == lax.broadcasted_iota(jnp.int32, (slots, slots), 1)
    total = dot(pick.astype(BF16), ycat[...])
    for copy in fetches:
        copy.wait()
    part = slots // len(stores)
    for i, store in enumerate(stores):
        at = slice(i * part, (i + 1) * part)
        for d in range(ncol):
            wide[pl.ds(i * part * ncol + d, part, stride=ncol), :] = total[
                at, d * nb : (d + 1) * nb
            ] + both[d, at, :].astype(F32)
        rows = slice(i * part * ncol, (i + 1) * part * ncol)
        packed[rows, :] = wide[rows, :].astype(BF16)
        store.start()
    for store in stores:
        store.wait()


def finish_kernel(occ_ref, z_ref, p_ref, base_ref, out_hbm, stage, sems, flat, middle, target):
    nslot, nvirt, nb = p_ref.shape
    ncol = nvirt // nb
    flat[: z_ref.shape[0], :] = z_ref[...].astype(F32)
    copies = [pltpu.make_async_copy(stage.at[s], out_hbm.at[s], sems.at[s]) for s in range(nslot)]

    def done(start, size):
        for s in range(start // ncol, (start + size) // ncol):
            for d in range(ncol):
                at = (s * ncol + d) * pitch_of(nb)
                rows = slice(d * nb, (d + 1) * nb)
                total = p_ref[s, rows, :].astype(F32) + target[at : at + nb, :]
                stage[s, rows, :] = total / (base_ref[rows, :] - occ_ref[s])
            copies[s].start()

    unskew(flat, middle, target, nb, nslot * ncol, done)
    for copy in copies:
        copy.wait()


SMEM = pl.BlockSpec(memory_space=pltpu.SMEM)
VMEM = pl.BlockSpec(memory_space=pltpu.VMEM)
HBM = pl.BlockSpec(memory_space=pltpu.HBM)


def stay(value):
    return pltpu.with_memory_space_constraint(value, pltpu.HBM)


def call(kernel, outs, scratch, specs, result=VMEM):
    return pl.pallas_call(
        kernel,
        out_shape=outs,
        in_specs=specs,
        out_specs=jax.tree.map(lambda _: result, outs),
        scratch_shapes=scratch,
        compiler_params=pltpu.CompilerParams(vmem_limit_bytes=20 << 20),
    )


def update_of(
    amplitudes,
    fock_left,
    dress_left,
    fock_right,
    dress_right,
    hole_ladder,
    slot_pair,
    partner,
    occ_energy,
    virt_energy,
    virt_order,
):
    slot_dev, nvirt, nb = amplitudes.shape
    slots = slot_pair.shape[0]
    npairs = hole_ladder.shape[0]
    nocc = occ_energy.shape[0]
    ncol = nvirt // nb
    count = slot_dev * ncol
    col = lax.axis_index("col")
    pair = lax.axis_index("pair")
    col_s = jnp.reshape(col, (1,)).astype(jnp.int32)
    pair_s = jnp.reshape(pair, (1,)).astype(jnp.int32)
    shape = jax.ShapeDtypeStruct

    def exchange(rows):
        sent = rows.reshape(nb * slot_dev, ncol, nb)
        got = lax.all_to_all(sent, "pair", split_axis=0, concat_axis=0, tiled=True)
        return got.reshape(nb * count, nb)

    def swap(value, k):
        return lax.ppermute(value, "col", [(i, i ^ k) for i in range(ncol)])

    far = swap(amplitudes, 2)
    dma = pltpu.SemaphoreType.DMA
    skewed = call(
        skew_kernel,
        shape((nb * count, nb), BF16),
        [
            pltpu.VMEM(amplitudes.shape, BF16),
            pltpu.VMEM((nb * count, nb), BF16),
            dma((slot_dev,)),
            dma((1 << split_bits(nb)[1],)),
        ]
        + skew_scratch(count, nb),
        [HBM],
        HBM,
    )(stay(amplitudes))
    x = exchange(skewed)
    pair_col = slot_pair.reshape(slots, 1)
    pair_row = slot_pair.reshape(1, slots)
    partner_col = partner.reshape(slots, 1)
    w, w2 = call(
        weights_kernel, [shape((slots, slots), BF16)] * 2, [], [VMEM] * 4
    )(pair_col, pair_row, partner_col, hole_ladder)
    near = swap(amplitudes, 1)
    both = swap(far, 1)
    wide = jnp.stack([fock_right, dress_right])
    wide_far = swap(wide, 2)
    wide_near = swap(wide, 1)
    wide_both = swap(wide_far, 1)
    particle_rows = call(
        rows_kernel,
        shape((nb * count, nb), BF16),
        [
            pltpu.VMEM((nb, 2 * nvirt), BF16),
            pltpu.VMEM((nvirt, nvirt), BF16),
            pltpu.VMEM((nvirt, nvirt), BF16),
            pltpu.VMEM((2 * nvirt, nvirt), BF16),
            pltpu.VMEM((nb, nvirt), BF16),
        ]
        + skew_scratch(count, nb),
        [SMEM] + [VMEM] * 10,
    )(
        col_s, amplitudes, near, far, both, wide, wide_near, wide_far, wide_both,
        fock_left, dress_left,
    )
    y = exchange(particle_rows)
    particle = call(
        cols_kernel,
        shape(amplitudes.shape, BF16),
        [pltpu.VMEM((nvirt, 2 * nb), BF16), pltpu.VMEM((nvirt, nvirt), BF16)],
        [SMEM] + [VMEM] * 7,
    )(col_s, amplitudes, near, far, both, wide, fock_left, dress_left)
    ladder, m0, m1, m2, m3 = call(
        ladder_kernel,
        [shape((ncol, slots, nb), BF16)] + [shape((slots, nb), BF16)] * 4,
        [
            pltpu.VMEM((slots * ncol, nb), F32),
            pltpu.VMEM((slots, nvirt), BF16),
            pltpu.VMEM((ncol, slots, nb), BF16),
        ],
        [SMEM] * 2 + [VMEM] * 3,
    )(col_s, pair_s, x, w, w2)
    m1, m2, m3 = swap(m1, 1), swap(m2, 2), swap(m3, 3)
    both_terms = call(
        mirror_kernel, shape((ncol, slots, nb), BF16), [], [SMEM] + [VMEM] * 5
    )(col_s, ladder, m0, m1, m2, m3)
    back = call(
        combine_kernel,
        shape((nb * count, nb), BF16),
        [
            pltpu.VMEM((slots * ncol, nb), F32),
            pltpu.VMEM((slots, nvirt), BF16),
            pltpu.VMEM((ncol, slots, nb), BF16),
            pltpu.VMEM((nb * count, nb), BF16),
            dma((ncol,)),
            dma((2,)),
        ],
        [VMEM, HBM, VMEM],
        HBM,
    )(y, stay(both_terms), partner_col)
    z = exchange(back)
    own_pairs = lax.dynamic_slice_in_dim(slot_pair, pair * slot_dev, slot_dev)
    occ_iota = jnp.arange(nocc, dtype=jnp.int32)
    first_hot = (own_pairs[:, None] // nocc == occ_iota[None, :]).astype(F32)
    second_hot = (own_pairs[:, None] % nocc == occ_iota[None, :]).astype(F32)
    live = (own_pairs < npairs).astype(F32)
    occ_sum = live * (
        jnp.sum(first_hot * occ_energy[None, :], axis=1)
        + jnp.sum(second_hot * occ_energy[None, :], axis=1)
    )
    virt_iota = jnp.arange(nvirt, dtype=jnp.int32)
    row_hot = (virt_order[:, None] == virt_iota[None, :]).astype(F32)
    row_energy = jnp.sum(row_hot * virt_energy[None, :], axis=1)
    col_energy = lax.dynamic_slice_in_dim(row_energy, col * nb, nb)
    base = row_energy[:, None] + col_energy[None, :]
    return call(
        finish_kernel,
        shape(amplitudes.shape, F32),
        [pltpu.VMEM(amplitudes.shape, F32), dma((slot_dev,))] + skew_scratch(count, nb),
        [SMEM] + [VMEM] * 3,
        HBM,
    )(occ_sum, z, particle, base)


def solution(mesh):
    placed = (
        P("pair", None, "col"),
        P(),
        P(),
        P(None, "col"),
        P(None, "col"),
        P(),
        P(),
        P(),
        P(),
        P(),
        P(),
    )
    return jax.shard_map(
        update_of, mesh=mesh, in_specs=placed, out_specs=P("pair", None, "col"), check_vma=False
    )
```

```python
import jax
import jax.numpy as jnp
from jax import lax
from jax.experimental import pallas as pl
from jax.experimental.pallas import tpu as pltpu
from jax.sharding import PartitionSpec as P

F32 = jnp.float32
BF16 = jnp.bfloat16
PAD = 8


def dot(left, right):
    return jnp.dot(left, right, preferred_element_type=F32)


def chunks_of(total):
    return [(start, min(8, total - start)) for start in range(0, total, 8)]


def pitch_of(nb):
    return nb + PAD


def swap_rows(values, bits, first_bit):
    for step in range(bits):
        take = ((lax.broadcasted_iota(jnp.int32, values[0].shape, 1) >> (first_bit + step)) & 1) == 1
        bit = 1 << step
        values = [jnp.where(take, values[i ^ bit], values[i]) for i in range(len(values))]
    return values


def split_bits(nb):
    total = nb.bit_length() - 1
    low = (total + 1) // 2
    return low, total - low


def skew(source, middle, target, nb, count, ready, done):
    low, high = split_bits(nb)
    pitch = pitch_of(nb)
    for start, size in chunks_of(count):
        ready(start, size)
        for base in range(1 << low):
            rows = [base + (i << low) for i in range(1 << high)]
            values = [source[pl.ds(start * pitch + r, size, stride=pitch), :] for r in rows]
            for r, value in zip(rows, swap_rows(values, high, low)):
                middle[r, start : start + size, :] = value
    for base in range(1 << high):
        rows = [(base << low) + i for i in range(1 << low)]
        for start, size in chunks_of(count):
            values = [middle[r, start : start + size, :] for r in rows]
            for r, value in zip(rows, swap_rows(values, low, 0)):
                target[r * count + start : r * count + start + size, :] = value
        done(rows[0] * count, len(rows) * count)


def unskew(source, middle, target, nb, count, done):
    low, high = split_bits(nb)
    pitch = pitch_of(nb)
    for start, size in chunks_of(count):
        for base in range(1 << low):
            rows = [base + (i << low) for i in range(1 << high)]
            values = [source[r * count + start : r * count + start + size, :] for r in rows]
            for r, value in zip(rows, swap_rows(values, high, low)):
                middle[r, start : start + size, :] = value
        for base in range(1 << high):
            rows = [(base << low) + i for i in range(1 << low)]
            values = [middle[r, start : start + size, :] for r in rows]
            for r, value in zip(rows, swap_rows(values, low, 0)):
                target[pl.ds(start * pitch + r, size, stride=pitch), :] = value
        done(start, size)


def pieces(source, target, sems, count):
    size = source.shape[0] // count
    return [
        pltpu.make_async_copy(
            source.at[pl.ds(i * size, size)], target.at[pl.ds(i * size, size)], sems.at[i]
        )
        for i in range(count)
    ]


def skew_kernel(a_hbm, out_hbm, raw, packed, sems_in, sems_out, flat, middle, target):
    nslot, nvirt, nb = raw.shape
    ncol = nvirt // nb
    fetches = pieces(a_hbm, raw, sems_in, nslot)
    for copy in fetches:
        copy.start()
    stores = pieces(packed, out_hbm, sems_out, sems_out.shape[0])

    def ready(start, size):
        for s in range(start // ncol, (start + size) // ncol):
            fetches[s].wait()
            for d in range(ncol):
                at = (s * ncol + d) * pitch_of(nb)
                flat[at : at + nb, :] = raw[s, d * nb : (d + 1) * nb, :].astype(F32)

    def done(start, size):
        packed[start : start + size, :] = target[start : start + size, :].astype(BF16)
        stores[start // size].start()

    skew(flat, middle, target, nb, nslot * ncol, ready, done)
    for copy in stores:
        copy.wait()


def skew_scratch(count, nb):
    return [
        pltpu.VMEM((count * pitch_of(nb), nb), F32),
        pltpu.VMEM((nb, -(-count // 8) * 8, nb), F32),
        pltpu.VMEM((count * pitch_of(nb), nb), F32),
    ]


def weights_kernel(pair_col, pair_row, partner_col, h_ref, w_ref, w2_ref):
    slots = w_ref.shape[0]
    npairs = h_ref.shape[0]
    pick = (pair_col[...] == lax.broadcasted_iota(jnp.int32, (slots, npairs), 1)).astype(BF16)
    pick_t = (pair_row[...] == lax.broadcasted_iota(jnp.int32, (npairs, slots), 0)).astype(BF16)
    half = dot(pick, h_ref[...]).astype(BF16)
    w = dot(half, pick_t).astype(BF16)
    w_ref[...] = w
    mirror = (partner_col[...] == lax.broadcasted_iota(jnp.int32, (slots, slots), 1)).astype(BF16)
    w2_ref[...] = dot(mirror, w).astype(BF16)


def gather_columns(parts, s, acat):
    nb = parts[0].shape[2]
    for k, part in enumerate(parts):
        acat[:, k * nb : (k + 1) * nb] = part[s]
    return acat[...]


def rows_kernel(
    c_ref, g0, g1, g2, g3, w0, w1, w2, w3, fl_ref, dl_ref, out_ref,
    left, dmat, fmat, stack, low, flat, middle, target,
):
    parts = (g0, g1, g2, g3)
    wide = (w0, w1, w2, w3)
    ncol = len(parts)
    nslot, nvirt, nb = g0.shape
    col = c_ref[0]
    own = pl.ds(pl.multiple_of(col * nb, nb), nb)
    left[:, :nvirt] = fl_ref[own, :]
    left[:, nvirt:] = dl_ref[own, :]
    for i in range(ncol):
        rows = pl.ds(pl.multiple_of((col ^ i) * nb, nb), nb)
        for k in range(ncol):
            at = (slice(i * nb, (i + 1) * nb), slice(k * nb, (k + 1) * nb))
            fmat[at] = wide[k][0, rows, :]
            dmat[at] = wide[k][1, rows, :]

    def ready(start, size):
        for s in range(start // ncol, (start + size) // ncol):
            for k, part in enumerate(parts):
                stack[:nvirt, k * nb : (k + 1) * nb] = part[s]
                low[:, k * nb : (k + 1) * nb] = part[s, own, :]
            stack[nvirt:, :] = dot(stack[:nvirt, :], dmat[...]).astype(BF16)
            total = dot(left[...], stack[...]) + dot(low[...], fmat[...])
            for k in range(ncol):
                at = pl.multiple_of((s * ncol + (col ^ k)) * pitch_of(nb), 8)
                flat[pl.ds(at, nb), :] = total[:, k * nb : (k + 1) * nb].T

    def done(start, size):
        out_ref[start : start + size, :] = target[start : start + size, :].astype(BF16)

    skew(flat, middle, target, nb, nslot * ncol, ready, done)


def cols_kernel(c_ref, g0, g1, g2, g3, w0, fl_ref, dl_ref, p_ref, right, acat):
    parts = (g0, g1, g2, g3)
    ncol = len(parts)
    nslot, _, nb = g0.shape
    col = c_ref[0]
    for i in range(ncol):
        rows = pl.ds(pl.multiple_of((col ^ i) * nb, nb), nb)
        right[i * nb : (i + 1) * nb, :nb] = w0[1, rows, :]
        right[i * nb : (i + 1) * nb, nb:] = w0[0, rows, :]
    for s in range(nslot):
        amp = gather_columns(parts, s, acat)
        both = dot(amp, right[...])
        dressed = both[:, :nb].astype(BF16)
        total = both[:, nb:] + dot(fl_ref[...], g0[s]) + dot(dl_ref[...], dressed)
        p_ref[s] = total.astype(BF16)


def ladder_kernel(c_ref, j_ref, x_ref, w_ref, w2_ref, l_ref, m0, m1, m2, m3, wide, xcat, mirror):
    slots = w_ref.shape[0]
    nb = x_ref.shape[1]
    ncol = x_ref.shape[0] // slots
    wide[...] = x_ref[...].astype(F32)
    for d in range(ncol):
        xcat[:, d * nb : (d + 1) * nb] = wide[pl.ds(d, slots, stride=ncol), :].astype(BF16)
    plain = dot(w_ref[...], xcat[...])
    for d in range(ncol):
        l_ref[d] = plain[:, d * nb : (d + 1) * nb].astype(BF16)
    other = dot(w2_ref[...], xcat[...]).astype(BF16)
    rows = lax.broadcasted_iota(jnp.int32, (nb, nb), 0)
    cols = lax.broadcasted_iota(jnp.int32, (nb, nb), 1)
    flip = (rows == (cols ^ j_ref[0])).astype(BF16)
    for d in range(ncol):
        mirror[d] = dot(other[:, d * nb : (d + 1) * nb], flip).astype(BF16)
    col = c_ref[0]
    for k, out in enumerate((m0, m1, m2, m3)):
        out[...] = mirror[col ^ k]


def mirror_kernel(c_ref, l_ref, m0, m1, m2, m3, out_ref):
    col = c_ref[0]
    for k, part in enumerate((m0, m1, m2, m3)):
        out_ref[col ^ k] = (l_ref[col ^ k].astype(F32) + part[...].astype(F32)).astype(BF16)


def combine_kernel(y_ref, both, partner_col, out_hbm, wide, ycat, packed, sems):
    ncol, slots, nb = both.shape
    stores = pieces(packed, out_hbm, sems, sems.shape[0])
    wide[...] = y_ref[...].astype(F32)
    for d in range(ncol):
        ycat[:, d * nb : (d + 1) * nb] = wide[pl.ds(d, slots, stride=ncol), :].astype(BF16)
    pick = partner_col[...] == lax.broadcasted_iota(jnp.int32, (slots, slots), 1)
    total = dot(pick.astype(BF16), ycat[...])
    part = slots // len(stores)
    for i, store in enumerate(stores):
        at = slice(i * part, (i + 1) * part)
        for d in range(ncol):
            wide[pl.ds(i * part * ncol + d, part, stride=ncol), :] = total[
                at, d * nb : (d + 1) * nb
            ] + both[d, at, :].astype(F32)
        rows = slice(i * part * ncol, (i + 1) * part * ncol)
        packed[rows, :] = wide[rows, :].astype(BF16)
        store.start()
    for store in stores:
        store.wait()


def finish_kernel(occ_ref, z_ref, p_ref, base_ref, out_hbm, stage, sems, flat, middle, target):
    nslot, nvirt, nb = p_ref.shape
    ncol = nvirt // nb
    flat[: z_ref.shape[0], :] = z_ref[...].astype(F32)
    copies = [pltpu.make_async_copy(stage.at[s], out_hbm.at[s], sems.at[s]) for s in range(nslot)]

    def done(start, size):
        for s in range(start // ncol, (start + size) // ncol):
            for d in range(ncol):
                at = (s * ncol + d) * pitch_of(nb)
                rows = slice(d * nb, (d + 1) * nb)
                total = p_ref[s, rows, :].astype(F32) + target[at : at + nb, :]
                stage[s, rows, :] = total / (base_ref[rows, :] - occ_ref[s])
            copies[s].start()

    unskew(flat, middle, target, nb, nslot * ncol, done)
    for copy in copies:
        copy.wait()


SMEM = pl.BlockSpec(memory_space=pltpu.SMEM)
VMEM = pl.BlockSpec(memory_space=pltpu.VMEM)
HBM = pl.BlockSpec(memory_space=pltpu.HBM)


def stay(value):
    return pltpu.with_memory_space_constraint(value, pltpu.HBM)


def call(kernel, outs, scratch, specs, result=VMEM):
    return pl.pallas_call(
        kernel,
        out_shape=outs,
        in_specs=specs,
        out_specs=jax.tree.map(lambda _: result, outs),
        scratch_shapes=scratch,
        compiler_params=pltpu.CompilerParams(vmem_limit_bytes=20 << 20),
    )


def update_of(
    amplitudes,
    fock_left,
    dress_left,
    fock_right,
    dress_right,
    hole_ladder,
    slot_pair,
    partner,
    occ_energy,
    virt_energy,
    virt_order,
):
    slot_dev, nvirt, nb = amplitudes.shape
    slots = slot_pair.shape[0]
    npairs = hole_ladder.shape[0]
    nocc = occ_energy.shape[0]
    ncol = nvirt // nb
    count = slot_dev * ncol
    col = lax.axis_index("col")
    pair = lax.axis_index("pair")
    col_s = jnp.reshape(col, (1,)).astype(jnp.int32)
    pair_s = jnp.reshape(pair, (1,)).astype(jnp.int32)
    shape = jax.ShapeDtypeStruct

    def exchange(rows):
        sent = rows.reshape(nb * slot_dev, ncol, nb)
        got = lax.all_to_all(sent, "pair", split_axis=0, concat_axis=0, tiled=True)
        return got.reshape(nb * count, nb)

    def swap(value, k):
        return lax.ppermute(value, "col", [(i, i ^ k) for i in range(ncol)])

    far = swap(amplitudes, 2)
    dma = pltpu.SemaphoreType.DMA
    skewed = call(
        skew_kernel,
        shape((nb * count, nb), BF16),
        [
            pltpu.VMEM(amplitudes.shape, BF16),
            pltpu.VMEM((nb * count, nb), BF16),
            dma((slot_dev,)),
            dma((1 << split_bits(nb)[1],)),
        ]
        + skew_scratch(count, nb),
        [HBM],
        HBM,
    )(stay(amplitudes))
    x = exchange(skewed)
    pair_col = slot_pair.reshape(slots, 1)
    pair_row = slot_pair.reshape(1, slots)
    partner_col = partner.reshape(slots, 1)
    w, w2 = call(
        weights_kernel, [shape((slots, slots), BF16)] * 2, [], [VMEM] * 4
    )(pair_col, pair_row, partner_col, hole_ladder)
    near = swap(amplitudes, 1)
    both = swap(far, 1)
    wide = jnp.stack([fock_right, dress_right])
    wide_far = swap(wide, 2)
    wide_near = swap(wide, 1)
    wide_both = swap(wide_far, 1)
    particle_rows = call(
        rows_kernel,
        shape((nb * count, nb), BF16),
        [
            pltpu.VMEM((nb, 2 * nvirt), BF16),
            pltpu.VMEM((nvirt, nvirt), BF16),
            pltpu.VMEM((nvirt, nvirt), BF16),
            pltpu.VMEM((2 * nvirt, nvirt), BF16),
            pltpu.VMEM((nb, nvirt), BF16),
        ]
        + skew_scratch(count, nb),
        [SMEM] + [VMEM] * 10,
    )(
        col_s, amplitudes, near, far, both, wide, wide_near, wide_far, wide_both,
        fock_left, dress_left,
    )
    y = exchange(particle_rows)
    particle = call(
        cols_kernel,
        shape(amplitudes.shape, BF16),
        [pltpu.VMEM((nvirt, 2 * nb), BF16), pltpu.VMEM((nvirt, nvirt), BF16)],
        [SMEM] + [VMEM] * 7,
    )(col_s, amplitudes, near, far, both, wide, fock_left, dress_left)
    ladder, m0, m1, m2, m3 = call(
        ladder_kernel,
        [shape((ncol, slots, nb), BF16)] + [shape((slots, nb), BF16)] * 4,
        [
            pltpu.VMEM((slots * ncol, nb), F32),
            pltpu.VMEM((slots, nvirt), BF16),
            pltpu.VMEM((ncol, slots, nb), BF16),
        ],
        [SMEM] * 2 + [VMEM] * 3,
    )(col_s, pair_s, x, w, w2)
    m1, m2, m3 = swap(m1, 1), swap(m2, 2), swap(m3, 3)
    both_terms = call(
        mirror_kernel, shape((ncol, slots, nb), BF16), [], [SMEM] + [VMEM] * 5
    )(col_s, ladder, m0, m1, m2, m3)
    back = call(
        combine_kernel,
        shape((nb * count, nb), BF16),
        [
            pltpu.VMEM((slots * ncol, nb), F32),
            pltpu.VMEM((slots, nvirt), BF16),
            pltpu.VMEM((nb * count, nb), BF16),
            dma((2,)),
        ],
        [VMEM, VMEM, VMEM],
        HBM,
    )(y, both_terms, partner_col)
    z = exchange(back)
    own_pairs = lax.dynamic_slice_in_dim(slot_pair, pair * slot_dev, slot_dev)
    occ_iota = jnp.arange(nocc, dtype=jnp.int32)
    first_hot = (own_pairs[:, None] // nocc == occ_iota[None, :]).astype(F32)
    second_hot = (own_pairs[:, None] % nocc == occ_iota[None, :]).astype(F32)
    live = (own_pairs < npairs).astype(F32)
    occ_sum = live * (
        jnp.sum(first_hot * occ_energy[None, :], axis=1)
        + jnp.sum(second_hot * occ_energy[None, :], axis=1)
    )
    virt_iota = jnp.arange(nvirt, dtype=jnp.int32)
    row_hot = (virt_order[:, None] == virt_iota[None, :]).astype(F32)
    row_energy = jnp.sum(row_hot * virt_energy[None, :], axis=1)
    col_energy = lax.dynamic_slice_in_dim(row_energy, col * nb, nb)
    base = row_energy[:, None] + col_energy[None, :]
    return call(
        finish_kernel,
        shape(amplitudes.shape, F32),
        [pltpu.VMEM(amplitudes.shape, F32), dma((slot_dev,))] + skew_scratch(count, nb),
        [SMEM] + [VMEM] * 3,
        HBM,
    )(occ_sum, z, particle, base)


def solution(mesh):
    placed = (
        P("pair", None, "col"),
        P(),
        P(),
        P(None, "col"),
        P(None, "col"),
        P(),
        P(),
        P(),
        P(),
        P(),
        P(),
    )
    return jax.shard_map(
        update_of, mesh=mesh, in_specs=placed, out_specs=P("pair", None, "col"), check_vma=False
    )
```

```python
import jax
import jax.numpy as jnp
from jax import lax
from jax.experimental import pallas as pl
from jax.experimental.pallas import tpu as pltpu
from jax.sharding import PartitionSpec as P

F32 = jnp.float32
BF16 = jnp.bfloat16
PAD = 8


def dot(left, right):
    return jnp.dot(left, right, preferred_element_type=F32)


def chunks_of(total):
    return [(start, min(8, total - start)) for start in range(0, total, 8)]


def pitch_of(nb):
    return nb + PAD


def swap_rows(values, bits, first_bit):
    for step in range(bits):
        take = ((lax.broadcasted_iota(jnp.int32, values[0].shape, 1) >> (first_bit + step)) & 1) == 1
        bit = 1 << step
        values = [jnp.where(take, values[i ^ bit], values[i]) for i in range(len(values))]
    return values


def split_bits(nb):
    total = nb.bit_length() - 1
    low = (total + 1) // 2
    return low, total - low


def skew(source, middle, target, nb, count, ready, done):
    low, high = split_bits(nb)
    pitch = pitch_of(nb)
    for start, size in chunks_of(count):
        ready(start, size)
        for base in range(1 << low):
            rows = [base + (i << low) for i in range(1 << high)]
            values = [source[pl.ds(start * pitch + r, size, stride=pitch), :] for r in rows]
            for r, value in zip(rows, swap_rows(values, high, low)):
                middle[r, start : start + size, :] = value
    for base in range(1 << high):
        rows = [(base << low) + i for i in range(1 << low)]
        for start, size in chunks_of(count):
            values = [middle[r, start : start + size, :] for r in rows]
            for r, value in zip(rows, swap_rows(values, low, 0)):
                target[r * count + start : r * count + start + size, :] = value
        done(rows[0] * count, len(rows) * count)


def unskew(source, middle, target, nb, count, done):
    low, high = split_bits(nb)
    pitch = pitch_of(nb)
    for start, size in chunks_of(count):
        for base in range(1 << low):
            rows = [base + (i << low) for i in range(1 << high)]
            values = [source[r * count + start : r * count + start + size, :] for r in rows]
            for r, value in zip(rows, swap_rows(values, high, low)):
                middle[r, start : start + size, :] = value
        for base in range(1 << high):
            rows = [(base << low) + i for i in range(1 << low)]
            values = [middle[r, start : start + size, :] for r in rows]
            for r, value in zip(rows, swap_rows(values, low, 0)):
                target[pl.ds(start * pitch + r, size, stride=pitch), :] = value
        done(start, size)


def pieces(source, target, sems, count):
    size = source.shape[0] // count
    return [
        pltpu.make_async_copy(
            source.at[pl.ds(i * size, size)], target.at[pl.ds(i * size, size)], sems.at[i]
        )
        for i in range(count)
    ]


def skew_kernel(a_hbm, out_hbm, raw, packed, sems_in, sems_out, flat, middle, target):
    nslot, nvirt, nb = raw.shape
    ncol = nvirt // nb
    fetches = pieces(a_hbm, raw, sems_in, nslot)
    for copy in fetches:
        copy.start()
    stores = pieces(packed, out_hbm, sems_out, sems_out.shape[0])

    def ready(start, size):
        for s in range(start // ncol, (start + size) // ncol):
            fetches[s].wait()
            for d in range(ncol):
                at = (s * ncol + d) * pitch_of(nb)
                flat[at : at + nb, :] = raw[s, d * nb : (d + 1) * nb, :].astype(F32)

    def done(start, size):
        packed[start : start + size, :] = target[start : start + size, :].astype(BF16)
        stores[start // size].start()

    skew(flat, middle, target, nb, nslot * ncol, ready, done)
    for copy in stores:
        copy.wait()


def skew_scratch(count, nb):
    return [
        pltpu.VMEM((count * pitch_of(nb), nb), F32),
        pltpu.VMEM((nb, -(-count // 8) * 8, nb), F32),
        pltpu.VMEM((count * pitch_of(nb), nb), F32),
    ]


def weights_kernel(pair_col, pair_row, partner_col, h_ref, w_ref, w2_ref):
    slots = w_ref.shape[0]
    npairs = h_ref.shape[0]
    pick = (pair_col[...] == lax.broadcasted_iota(jnp.int32, (slots, npairs), 1)).astype(BF16)
    pick_t = (pair_row[...] == lax.broadcasted_iota(jnp.int32, (npairs, slots), 0)).astype(BF16)
    half = dot(pick, h_ref[...]).astype(BF16)
    w = dot(half, pick_t).astype(BF16)
    w_ref[...] = w
    mirror = (partner_col[...] == lax.broadcasted_iota(jnp.int32, (slots, slots), 1)).astype(BF16)
    w2_ref[...] = dot(mirror, w).astype(BF16)


def gather_columns(parts, s, acat):
    nb = parts[0].shape[2]
    for k, part in enumerate(parts):
        acat[:, k * nb : (k + 1) * nb] = part[s]
    return acat[...]


def rows_kernel(
    c_ref, g0, g1, g2, g3, w0, w1, w2, w3, fl_ref, dl_ref, out_ref,
    left, dmat, fmat, stack, low, flat, middle, target,
):
    parts = (g0, g1, g2, g3)
    wide = (w0, w1, w2, w3)
    ncol = len(parts)
    nslot, nvirt, nb = g0.shape
    col = c_ref[0]
    own = pl.ds(pl.multiple_of(col * nb, nb), nb)
    left[:, :nvirt] = fl_ref[own, :]
    left[:, nvirt:] = dl_ref[own, :]
    for i in range(ncol):
        rows = pl.ds(pl.multiple_of((col ^ i) * nb, nb), nb)
        for k in range(ncol):
            at = (slice(i * nb, (i + 1) * nb), slice(k * nb, (k + 1) * nb))
            fmat[at] = wide[k][0, rows, :]
            dmat[at] = wide[k][1, rows, :]

    def ready(start, size):
        for s in range(start // ncol, (start + size) // ncol):
            for k, part in enumerate(parts):
                stack[:nvirt, k * nb : (k + 1) * nb] = part[s]
                low[:, k * nb : (k + 1) * nb] = part[s, own, :]
            stack[nvirt:, :] = dot(stack[:nvirt, :], dmat[...]).astype(BF16)
            total = dot(left[...], stack[...]) + dot(low[...], fmat[...])
            for k in range(ncol):
                at = pl.multiple_of((s * ncol + (col ^ k)) * pitch_of(nb), 8)
                flat[pl.ds(at, nb), :] = total[:, k * nb : (k + 1) * nb].T

    def done(start, size):
        out_ref[start : start + size, :] = target[start : start + size, :].astype(BF16)

    skew(flat, middle, target, nb, nslot * ncol, ready, done)


def cols_kernel(c_ref, g0, g1, g2, g3, w0, fl_ref, dl_ref, p_ref, right, acat):
    parts = (g0, g1, g2, g3)
    ncol = len(parts)
    nslot, _, nb = g0.shape
    col = c_ref[0]
    for i in range(ncol):
        rows = pl.ds(pl.multiple_of((col ^ i) * nb, nb), nb)
        right[i * nb : (i + 1) * nb, :nb] = w0[1, rows, :]
        right[i * nb : (i + 1) * nb, nb:] = w0[0, rows, :]
    for s in range(nslot):
        amp = gather_columns(parts, s, acat)
        both = dot(amp, right[...])
        dressed = both[:, :nb].astype(BF16)
        total = both[:, nb:] + dot(fl_ref[...], g0[s]) + dot(dl_ref[...], dressed)
        p_ref[s] = total.astype(BF16)


def ladder_kernel(c_ref, j_ref, x_ref, w_ref, w2_ref, l_ref, m0, m1, m2, m3, wide, xcat, mirror):
    slots = w_ref.shape[0]
    nb = x_ref.shape[1]
    ncol = x_ref.shape[0] // slots
    wide[...] = x_ref[...].astype(F32)
    for d in range(ncol):
        xcat[:, d * nb : (d + 1) * nb] = wide[pl.ds(d, slots, stride=ncol), :].astype(BF16)
    plain = dot(w_ref[...], xcat[...])
    for d in range(ncol):
        l_ref[d] = plain[:, d * nb : (d + 1) * nb].astype(BF16)
    other = dot(w2_ref[...], xcat[...]).astype(BF16)
    rows = lax.broadcasted_iota(jnp.int32, (nb, nb), 0)
    cols = lax.broadcasted_iota(jnp.int32, (nb, nb), 1)
    flip = (rows == (cols ^ j_ref[0])).astype(BF16)
    for d in range(ncol):
        mirror[d] = dot(other[:, d * nb : (d + 1) * nb], flip).astype(BF16)
    col = c_ref[0]
    for k, out in enumerate((m0, m1, m2, m3)):
        out[...] = mirror[col ^ k]


def mirror_kernel(c_ref, l_ref, m0, m1, m2, m3, out_ref):
    col = c_ref[0]
    for k, part in enumerate((m0, m1, m2, m3)):
        out_ref[col ^ k] = (l_ref[col ^ k].astype(F32) + part[...].astype(F32)).astype(BF16)


def combine_kernel(y_ref, both, partner_col, out_hbm, wide, ycat, packed, sems):
    ncol, slots, nb = both.shape
    stores = pieces(packed, out_hbm, sems, sems.shape[0])
    wide[...] = y_ref[...].astype(F32)
    for d in range(ncol):
        ycat[:, d * nb : (d + 1) * nb] = wide[pl.ds(d, slots, stride=ncol), :].astype(BF16)
    pick = partner_col[...] == lax.broadcasted_iota(jnp.int32, (slots, slots), 1)
    total = dot(pick.astype(BF16), ycat[...])
    part = slots // len(stores)
    for i, store in enumerate(stores):
        at = slice(i * part, (i + 1) * part)
        for d in range(ncol):
            wide[pl.ds(i * part * ncol + d, part, stride=ncol), :] = total[
                at, d * nb : (d + 1) * nb
            ] + both[d, at, :].astype(F32)
        rows = slice(i * part * ncol, (i + 1) * part * ncol)
        packed[rows, :] = wide[rows, :].astype(BF16)
        store.start()
    for store in stores:
        store.wait()


def finish_kernel(occ_ref, z_ref, p_ref, base_ref, out_hbm, stage, sems, flat, middle, target):
    nslot, nvirt, nb = p_ref.shape
    ncol = nvirt // nb
    flat[: z_ref.shape[0], :] = z_ref[...].astype(F32)
    copies = []
    for block in range(nslot * ncol):
        s, rows = block // ncol, pl.ds(block % ncol * nb, nb)
        copies.append(
            pltpu.make_async_copy(stage.at[s, rows], out_hbm.at[s, rows], sems.at[block])
        )

    def done(start, size):
        for s in range(start // ncol, (start + size) // ncol):
            for d in range(ncol):
                at = (s * ncol + d) * pitch_of(nb)
                rows = slice(d * nb, (d + 1) * nb)
                total = p_ref[s, rows, :].astype(F32) + target[at : at + nb, :]
                stage[s, rows, :] = total / (base_ref[rows, :] - occ_ref[s])
                copies[s * ncol + d].start()

    unskew(flat, middle, target, nb, nslot * ncol, done)
    for copy in copies:
        copy.wait()


SMEM = pl.BlockSpec(memory_space=pltpu.SMEM)
VMEM = pl.BlockSpec(memory_space=pltpu.VMEM)
HBM = pl.BlockSpec(memory_space=pltpu.HBM)


def stay(value):
    return pltpu.with_memory_space_constraint(value, pltpu.HBM)


def call(kernel, outs, scratch, specs, result=VMEM):
    return pl.pallas_call(
        kernel,
        out_shape=outs,
        in_specs=specs,
        out_specs=jax.tree.map(lambda _: result, outs),
        scratch_shapes=scratch,
        compiler_params=pltpu.CompilerParams(vmem_limit_bytes=20 << 20),
    )


def update_of(
    amplitudes,
    fock_left,
    dress_left,
    fock_right,
    dress_right,
    hole_ladder,
    slot_pair,
    partner,
    occ_energy,
    virt_energy,
    virt_order,
):
    slot_dev, nvirt, nb = amplitudes.shape
    slots = slot_pair.shape[0]
    npairs = hole_ladder.shape[0]
    nocc = occ_energy.shape[0]
    ncol = nvirt // nb
    count = slot_dev * ncol
    col = lax.axis_index("col")
    pair = lax.axis_index("pair")
    col_s = jnp.reshape(col, (1,)).astype(jnp.int32)
    pair_s = jnp.reshape(pair, (1,)).astype(jnp.int32)
    shape = jax.ShapeDtypeStruct

    def exchange(rows):
        sent = rows.reshape(nb * slot_dev, ncol, nb)
        got = lax.all_to_all(sent, "pair", split_axis=0, concat_axis=0, tiled=True)
        return got.reshape(nb * count, nb)

    def swap(value, k):
        return lax.ppermute(value, "col", [(i, i ^ k) for i in range(ncol)])

    far = swap(amplitudes, 2)
    dma = pltpu.SemaphoreType.DMA
    skewed = call(
        skew_kernel,
        shape((nb * count, nb), BF16),
        [
            pltpu.VMEM(amplitudes.shape, BF16),
            pltpu.VMEM((nb * count, nb), BF16),
            dma((slot_dev,)),
            dma((1 << split_bits(nb)[1],)),
        ]
        + skew_scratch(count, nb),
        [HBM],
        HBM,
    )(stay(amplitudes))
    x = exchange(skewed)
    pair_col = slot_pair.reshape(slots, 1)
    pair_row = slot_pair.reshape(1, slots)
    partner_col = partner.reshape(slots, 1)
    w, w2 = call(
        weights_kernel, [shape((slots, slots), BF16)] * 2, [], [VMEM] * 4
    )(pair_col, pair_row, partner_col, hole_ladder)
    near = swap(amplitudes, 1)
    both = swap(far, 1)
    wide = jnp.stack([fock_right, dress_right])
    wide_far = swap(wide, 2)
    wide_near = swap(wide, 1)
    wide_both = swap(wide_far, 1)
    particle_rows = call(
        rows_kernel,
        shape((nb * count, nb), BF16),
        [
            pltpu.VMEM((nb, 2 * nvirt), BF16),
            pltpu.VMEM((nvirt, nvirt), BF16),
            pltpu.VMEM((nvirt, nvirt), BF16),
            pltpu.VMEM((2 * nvirt, nvirt), BF16),
            pltpu.VMEM((nb, nvirt), BF16),
        ]
        + skew_scratch(count, nb),
        [SMEM] + [VMEM] * 10,
    )(
        col_s, amplitudes, near, far, both, wide, wide_near, wide_far, wide_both,
        fock_left, dress_left,
    )
    y = exchange(particle_rows)
    particle = call(
        cols_kernel,
        shape(amplitudes.shape, BF16),
        [pltpu.VMEM((nvirt, 2 * nb), BF16), pltpu.VMEM((nvirt, nvirt), BF16)],
        [SMEM] + [VMEM] * 7,
    )(col_s, amplitudes, near, far, both, wide, fock_left, dress_left)
    ladder, m0, m1, m2, m3 = call(
        ladder_kernel,
        [shape((ncol, slots, nb), BF16)] + [shape((slots, nb), BF16)] * 4,
        [
            pltpu.VMEM((slots * ncol, nb), F32),
            pltpu.VMEM((slots, nvirt), BF16),
            pltpu.VMEM((ncol, slots, nb), BF16),
        ],
        [SMEM] * 2 + [VMEM] * 3,
    )(col_s, pair_s, x, w, w2)
    m1, m2, m3 = swap(m1, 1), swap(m2, 2), swap(m3, 3)
    both_terms = call(
        mirror_kernel, shape((ncol, slots, nb), BF16), [], [SMEM] + [VMEM] * 5
    )(col_s, ladder, m0, m1, m2, m3)
    back = call(
        combine_kernel,
        shape((nb * count, nb), BF16),
        [
            pltpu.VMEM((slots * ncol, nb), F32),
            pltpu.VMEM((slots, nvirt), BF16),
            pltpu.VMEM((nb * count, nb), BF16),
            dma((2,)),
        ],
        [VMEM, VMEM, VMEM],
        HBM,
    )(y, both_terms, partner_col)
    z = exchange(back)
    own_pairs = lax.dynamic_slice_in_dim(slot_pair, pair * slot_dev, slot_dev)
    occ_iota = jnp.arange(nocc, dtype=jnp.int32)
    first_hot = (own_pairs[:, None] // nocc == occ_iota[None, :]).astype(F32)
    second_hot = (own_pairs[:, None] % nocc == occ_iota[None, :]).astype(F32)
    live = (own_pairs < npairs).astype(F32)
    occ_sum = live * (
        jnp.sum(first_hot * occ_energy[None, :], axis=1)
        + jnp.sum(second_hot * occ_energy[None, :], axis=1)
    )
    virt_iota = jnp.arange(nvirt, dtype=jnp.int32)
    row_hot = (virt_order[:, None] == virt_iota[None, :]).astype(F32)
    row_energy = jnp.sum(row_hot * virt_energy[None, :], axis=1)
    col_energy = lax.dynamic_slice_in_dim(row_energy, col * nb, nb)
    base = row_energy[:, None] + col_energy[None, :]
    return call(
        finish_kernel,
        shape(amplitudes.shape, F32),
        [pltpu.VMEM(amplitudes.shape, F32), dma((count,))] + skew_scratch(count, nb),
        [SMEM] + [VMEM] * 3,
        HBM,
    )(occ_sum, z, particle, base)


def solution(mesh):
    placed = (
        P("pair", None, "col"),
        P(),
        P(),
        P(None, "col"),
        P(None, "col"),
        P(),
        P(),
        P(),
        P(),
        P(),
        P(),
    )
    return jax.shard_map(
        update_of, mesh=mesh, in_specs=placed, out_specs=P("pair", None, "col"), check_vma=False
    )
```
